256 devices in a mesh: space: 32 (over x, z), tile: 8 (over y, core).
Axes of the slice: x: 4, y: 4, z: 8, core: 2. Of those that a mesh axis runs over, the one named last changes fastest.
Arguments:
- eigenvectors: float32 [2, 256, 3, 262144], P(None, None, None, ('space', 'tile')), may hold values from -6 to 6
- perambulator: float32 [2, 1024, 1024], P(None, 'space'), may hold values from -6 to 6
- momenta: int32 [2, 3], replicated, may hold values from 1 to 2
- graph_blocks: int32 [256, 2], replicated, may hold values from 0 to 15
Outputs:
- elementals: float32 [2, 2, 256, 256], P(None, None, 'tile', 'space')
- contractions: float32 [256, 2, 128, 128], P(('space', 'tile'))
The draws below stay inside these ranges and needn't reach their ends.
All inputs are finite; a program needn't handle non-finite values.
Results may differ from the reference program's by a relative error of at most 0.00016.
Values sent between devices are 32-bit elements; how exact they have to be, the bound alone decides.
A program may use at most 64 MiB of HBM per device.

```python
import math
import jax
import jax.numpy as jnp
import numpy as np
from jax import lax

NEV = 256
NC = 3
NMOM = 2
SITES_DEV = 1024
SITES = 262144
ORDER = 1024
BLOCK = 128
NBLK = 16
NGRAPH = 256
N_TILE = 8
DEVICES = 256


def set_ends(array, key, low, high):
    dims = array.shape
    place = [jax.random.randint(jax.random.fold_in(key, axis), (), 0, dims[axis]) for axis in range(len(dims))]
    array = array.at[tuple(place)].set(low)
    longest = dims.index(max(dims))
    place[longest] = (place[longest] + 1) % dims[longest]
    return array.at[tuple(place)].set(high)


def block_scale(key, shape, pieces, smallest, high):
    gain = 1.0
    for dim, shards_of in pieces:
        steps = jax.random.uniform(jax.random.fold_in(jax.random.fold_in(key, 6), dim), (shards_of,), jnp.float32, smallest / len(pieces), high / len(pieces))
        gain = gain * jnp.repeat(jnp.exp(steps), shape[dim] // shards_of).reshape((-1,) + (1,) * (len(shape) - 1 - dim))
    return gain


def rank_table(amount, lean):
    loads = [(1 << 20) // math.isqrt(standing ** lean) + 1 for standing in range(1, amount + 1)]
    scale = 1 + sum(loads) // (1 << 30)
    return np.cumsum(np.array([max(1, weight // scale) for weight in loads]))


def ranked(own_key, dims, count, skew):
    listing = rank_table(count, skew)
    pick = jax.random.randint(jax.random.fold_in(own_key, 1), dims, 0, int(listing[count - 1]))
    grade = jnp.searchsorted(jnp.asarray(listing, jnp.int32), pick, side="right")
    return jax.random.permutation(jax.random.fold_in(own_key, 2), count)[grade].astype(jnp.int32)


def bell_draw(stream_key, extent, deviation, bound, pieces=(), kind=jnp.bfloat16):
    values = deviation * jax.random.normal(stream_key, extent, jnp.float32)
    if pieces:
        values = values * block_scale(stream_key, extent, pieces, -0.22, 0.18)
    return jnp.clip(values, -bound, bound).astype(kind)


def setup_inputs(seed: int = 0) -> dict:
    key_list = jax.random.split(jax.random.key(seed), 5)
    return {
        "eigenvectors": bell_draw(key_list[0], (2, NEV, NC, SITES), 1.0, 6.0, ((3, 256),), jnp.float32),
        "perambulator": bell_draw(key_list[1], (2, ORDER, ORDER), 1.0, 6.0, ((1, 32),), jnp.float32),
        "momenta": set_ends(jax.random.randint(key_list[2], (NMOM, 3), 1, 3), jax.random.fold_in(key_list[2], 1), 1, 2).astype(jnp.int32),
        "graph_blocks": set_ends(ranked(key_list[3], (NGRAPH, 2), NBLK, 2), jax.random.fold_in(key_list[3], 3), 0, NBLK - 1).astype(jnp.int32),
    }


lattice_edge = 64

def inner_product(left, right):
    return lax.dot_general(left, right, (((1,), (1,)), ((), ())), precision=lax.Precision.HIGHEST, preferred_element_type=jnp.float32)

def phased_gram(vectors, momenta, first_site):
    vector_count = vectors.shape[1]
    site_index = first_site + lax.iota(jnp.int32, vectors.shape[3])
    x_pos = site_index % lattice_edge
    y_pos = site_index // lattice_edge % lattice_edge
    z_pos = site_index // (lattice_edge * lattice_edge)
    wave_number = (momenta[:, 0:1] * x_pos[None, :] + momenta[:, 1:2] * y_pos[None, :] + momenta[:, 2:3] * z_pos[None, :]) % lattice_edge
    phase_angle = wave_number.astype(jnp.float32) * (2.0 * math.pi / lattice_edge)
    cosine = jnp.cos(phase_angle)
    sine_part = jnp.sin(phase_angle)
    real_part = vectors[0]
    imag_part = vectors[1]
    flat_real = real_part.reshape(vector_count, -1)
    flat_imag = imag_part.reshape(vector_count, -1)
    stacked = []
    for moment in range(momenta.shape[0]):
        cos_row = cosine[moment][None, None, :]
        sin_row = sine_part[moment][None, None, :]
        phased_real = (cos_row * real_part + sin_row * imag_part).reshape(vector_count, -1)
        phased_imag = (cos_row * imag_part - sin_row * real_part).reshape(vector_count, -1)
        gram_real = inner_product(flat_real, phased_real) + inner_product(flat_imag, phased_imag)
        gram_imag = inner_product(flat_real, phased_imag) - inner_product(flat_imag, phased_real)
        stacked.append(jnp.stack([gram_real, gram_imag]))
    return jnp.stack(stacked)

def transport(elementals_rows, perambulator_part):
    sources = perambulator_part.shape[1]
    vector_count = elementals_rows.shape[3]
    tensor = perambulator_part.reshape(2, sources, vector_count, -1)

    def apply_part(tau_part, phi_part):
        return jnp.einsum('cja,mij->mcia', tau_part, phi_part, precision=lax.Precision.HIGHEST, preferred_element_type=jnp.float32)
    mixed_real = apply_part(tensor[0], elementals_rows[:, 0]) - apply_part(tensor[1], elementals_rows[:, 1])
    mixed_imag = apply_part(tensor[0], elementals_rows[:, 1]) + apply_part(tensor[1], elementals_rows[:, 0])
    row_total = elementals_rows.shape[2] * tensor.shape[3]
    result = jnp.stack([mixed_real, mixed_imag], axis=1)
    return result.reshape(result.shape[0], 2, sources, row_total) * (1.0 / math.sqrt(vector_count))

def pair_product(left, right):

    def contract(first, second):
        return jnp.einsum('gcr,gcs->grs', first, second, precision=lax.Precision.HIGHEST, preferred_element_type=jnp.float32)
    pair_real = contract(left[:, 0], right[:, 0]) - contract(left[:, 1], right[:, 1])
    pair_imag = contract(left[:, 0], right[:, 1]) + contract(left[:, 1], right[:, 0])
    return jnp.stack([pair_real, pair_imag], axis=1)

def reference(eigenvectors, perambulator, momenta, graph_blocks):

    def accumulate(block_index, total):
        first_site = block_index.astype(jnp.int32) * SITES_DEV
        piece = lax.dynamic_slice_in_dim(eigenvectors, first_site, SITES_DEV, 3)
        return total + phased_gram(piece, momenta, first_site)
    gram = lax.fori_loop(0, DEVICES, accumulate, jnp.zeros((NMOM, 2, NEV, NEV), jnp.float32))
    elementals = gram * (1.0 / math.sqrt(NC * SITES))
    mixed_rows = transport(elementals, perambulator)
    blocks = mixed_rows.reshape(NMOM, 2, ORDER, N_TILE, BLOCK).transpose(0, 3, 1, 2, 4).reshape(NBLK, 2, ORDER, BLOCK)

    def one_graph(pair_ids):
        left = lax.dynamic_index_in_dim(blocks, pair_ids[0], 0, keepdims=True)
        right = lax.dynamic_index_in_dim(blocks, pair_ids[1], 0, keepdims=True)
        return pair_product(left, right)[0]
    contractions = lax.map(one_graph, graph_blocks) * (1.0 / math.sqrt(ORDER))
    return (elementals, contractions)
```

```python
import math

import jax
import jax.numpy as jnp
from jax import lax
from jax.sharding import PartitionSpec as P

NEV = 256
NC = 3
SPIN = 4
NMOM = 2
EDGE = 64
HIGH = lax.Precision.HIGH


def gram(vectors, momenta, first_site):
    site = first_site + lax.iota(jnp.int32, vectors.shape[3])
    x, y, z = site % EDGE, site // EDGE % EDGE, site // (EDGE * EDGE)
    wave = (momenta[:, 0:1] * x + momenta[:, 1:2] * y + momenta[:, 2:3] * z) % EDGE
    angle = wave.astype(jnp.float32) * (2.0 * math.pi / EDGE)
    cosine, sine = jnp.cos(angle), jnp.sin(angle)
    real, imag = vectors[0], vectors[1]

    def dot(a, b):
        return lax.dot_general(
            a,
            b,
            (((1, 2), (1, 2)), ((), ())),
            precision=HIGH,
            preferred_element_type=jnp.float32,
        )

    out = []
    for p in range(NMOM):
        c, s = cosine[p][None, None, :], sine[p][None, None, :]
        pr = c * real + s * imag
        pi = c * imag - s * real
        rr = dot(real, pr)
        ii = dot(imag, pi)
        mixed = dot(real - imag, pr + pi)
        out.append(jnp.stack([rr + ii, mixed - rr + ii]))
    return jnp.stack(out)


def per_device(eigenvectors, perambulator, momenta, graph_blocks):
    tiles = lax.axis_size("tile")
    spaces = lax.axis_size("space")
    space, tile = lax.axis_index("space"), lax.axis_index("tile")
    sites = eigenvectors.shape[3]
    mine = space * tiles + tile
    norm = 1.0 / math.sqrt(NC * sites * spaces * tiles)
    tau = perambulator.reshape(2, -1, NEV, SPIN).transpose(0, 3, 1, 2)
    tau = lax.all_gather(tau, "space", axis=2, tiled=True)
    phi = lax.psum(gram(eigenvectors, momenta, mine * sites) * norm, ("space", "tile"))
    rows, cols = NEV // tiles, NEV // spaces
    elementals = lax.dynamic_slice(phi, (0, 0, tile * rows, space * cols), (NMOM, 2, rows, cols))
    pair = lax.dynamic_slice(graph_blocks, (mine, 0), (1, 2))[0]
    by_block = phi.reshape(NMOM, 2, tiles, rows, NEV).transpose(0, 2, 1, 3, 4).reshape(-1, 2, rows, NEV)
    picked = by_block[pair]

    def apply(tau_part, phi_part):
        return jnp.einsum(
            "akj,bij->bkia", tau_part, phi_part, precision=HIGH, preferred_element_type=jnp.float32
        )

    re = apply(tau[0], picked[:, 0]) - apply(tau[1], picked[:, 1])
    im = apply(tau[0], picked[:, 1]) + apply(tau[1], picked[:, 0])
    scale = 1.0 / math.sqrt(NEV)
    re = (re * scale).reshape(2, re.shape[1], -1)
    im = (im * scale).reshape(2, im.shape[1], -1)

    def contract(a, b):
        return lax.dot_general(
            a, b, (((0,), (0,)), ((), ())), precision=HIGH, preferred_element_type=jnp.float32
        )

    out_re = contract(re[0], re[1]) - contract(im[0], im[1])
    out_im = contract(re[0], im[1]) + contract(im[0], re[1])
    contractions = jnp.stack([out_re, out_im])[None] * (1.0 / math.sqrt(SPIN * NEV))
    return elementals, contractions


def solution(mesh):
    return jax.shard_map(
        per_device,
        mesh=mesh,
        in_specs=(P(None, None, None, ("space", "tile")), P(None, "space", None), P(), P()),
        out_specs=(P(None, None, "tile", "space"), P(("space", "tile"), None, None, None)),
        check_vma=False,
    )
```

```python
import functools
import math

import jax
import jax.numpy as jnp
from jax import lax
from jax.experimental import pallas as pl
from jax.experimental.pallas import tpu as pltpu
from jax.sharding import PartitionSpec as P

NEV = 256
NC = 3
SPIN = 4
NMOM = 2
EDGE = 64
NX, NY, NZ = 4, 4, 8
PLANE = NX * NY
RANKS = 2 * PLANE
NSPACE = NX * NZ
MESH = pl.DeviceIdType.MESH
F32 = jnp.float32
BF16 = jnp.bfloat16
NT = (((1,), (1,)), ((), ()))
TN = (((0,), (0,)), ((), ()))


def split(v):
    hi = v.astype(BF16)
    return hi, (v - hi.astype(F32)).astype(BF16)


def dot(a, b, dims=NT):
    return lax.dot_general(a, b, dims, preferred_element_type=F32)


def kernel(
    momenta, graphs, eig, tau_in, el_ref, out_ref,
    vec, left, trig, acc, ebuf, stage, pair_in, plane_in, line_in, full, pick, picked, rows, rowed,
    tau, tau_hi, tau_lo,
    load_sem, own_sem, pair_send, pair_recv, plane_send, plane_recv, line_send, line_recv,
    pick_send, pick_recv, rows_send, rows_recv,
    ax_send, ax_recv, az_send, az_recv, bz_send, bz_recv, bx_send, bx_recv, push_send, push_recv,
):
    space, tile = lax.axis_index("space"), lax.axis_index("tile")
    x, z = space // NZ, space % NZ
    y, core = tile // 2, tile % 2
    place = x * NY + y
    rank = core * PLANE + place
    me = space * (2 * NY) + tile
    sites = vec.shape[3]

    def at_plane(other_rank):
        c, q = other_rank // PLANE, other_rank % PLANE
        return ((q // NY) * NZ + z, (q % NY) * 2 + c)

    def at_z(zz):
        return (x * NZ + zz, tile)

    def at_x(xx):
        return (xx * NZ + z, tile)

    partner = (space, y * 2 + 1 - core)

    def remote(src, dst, send, recv, device):
        return pltpu.make_async_remote_copy(
            src_ref=src, dst_ref=dst, send_sem=send, recv_sem=recv, device_id=device, device_id_type=MESH
        )

    barrier = pltpu.get_barrier_semaphore()

    def greet(j, _):
        pl.semaphore_signal(barrier, inc=1, device_id=at_plane((rank + j) % RANKS), device_id_type=MESH)
        return 0

    lax.fori_loop(1, RANKS, greet, 0)

    def greet_z(j, _):
        pl.semaphore_signal(barrier, inc=1, device_id=at_z((z + j) % NZ), device_id_type=MESH)
        return 0

    lax.fori_loop(1, NZ, greet_z, 0)

    loads = [pltpu.make_async_copy(eig.at[:, c], vec.at[:, c], load_sem.at[c]) for c in range(NC)]
    for load in loads:
        load.start()
    a_a, a_b = 2 * core, 2 * core + 1
    slot = z * NX + x
    own = [
        pltpu.make_async_copy(tau_in.at[a_a], tau.at[a_a, slot], own_sem.at[0]),
        pltpu.make_async_copy(tau_in.at[a_b], tau.at[a_b, slot], own_sem.at[1]),
    ]
    for copy in own:
        copy.start()

    site = me * sites + lax.broadcasted_iota(jnp.int32, (1, sites), 1)
    px, py, pz = site & (EDGE - 1), (site >> 6) & (EDGE - 1), site >> 12
    for p in range(NMOM):
        wave = (momenta[p, 0] * px + momenta[p, 1] * py + momenta[p, 2] * pz) & (EDGE - 1)
        angle = wave.astype(F32) * (2.0 * math.pi / EDGE)
        trig[p, 0:1, :] = jnp.cos(angle)
        trig[p, 1:2, :] = jnp.sin(angle)

    pl.semaphore_wait(barrier, RANKS - 1 + NZ - 1)

    started = []

    def go(copy):
        copy.start()
        started.append(copy)

    def bundle(a, zz):
        return tau.at[a, pl.ds(zz * NX, NX)]

    def half_bundle(a, zz, h):
        return tau.at[a, pl.ds(zz * NX + h * (NX // 2), NX // 2)]

    def push(a, zz, k):
        go(remote(bundle(a, zz), bundle(a, zz), push_send.at[k], push_recv.at[k], partner))

    def waits(ref, sem):
        pltpu.make_async_copy(ref, ref, sem).wait()

    def b_along_x(zz, k):
        for j in range(1, NX):
            ref = tau.at[a_b, zz * NX + x]
            go(remote(ref, ref, bx_send.at[k, j - 1], bx_recv.at[k], at_x((x + j) % NX)))

    def z_back(h):
        return (z + NZ - h) % NZ

    def z_on(h):
        return (z + h) % NZ

    def tau_first():
        own[0].wait()
        own[1].wait()
        for j in range(1, NX):
            ref = tau.at[a_a, slot]
            go(remote(ref, ref, ax_send.at[j - 1], ax_recv.at[0], at_x((x + j) % NX)))
        ref = tau.at[a_b, slot]
        go(remote(ref, ref, bz_send.at[0, 0], bz_recv.at[0, 0], at_z(z_on(1))))
        go(remote(ref, ref, bz_send.at[1, 0], bz_recv.at[1, 0], at_z(z_back(1))))
        b_along_x(z, 0)

    def b_z(h):
        up, down = z_back(h), z_on(h)
        ref_up, ref_down = tau.at[a_b, up * NX + x], tau.at[a_b, down * NX + x]
        if h < NZ // 2:
            waits(ref_up, bz_recv.at[0, h - 1])
            waits(ref_down, bz_recv.at[1, h - 1])
            if h + 1 == NZ // 2:
                ref_u, ref_d = ref_up.at[0], ref_down.at[1]
            else:
                ref_u, ref_d = ref_up, ref_down
            go(remote(ref_u, ref_u, bz_send.at[0, h], bz_recv.at[0, h], at_z(z_on(1))))
            go(remote(ref_d, ref_d, bz_send.at[1, h], bz_recv.at[1, h], at_z(z_back(1))))
            b_along_x(up, h)
            b_along_x(down, NZ // 2 + h)
        else:
            waits(ref_up.at[0], bz_recv.at[0, h - 1])
            waits(ref_up.at[1], bz_recv.at[1, h - 1])
            b_along_x(up, h)

    def b_push(k):
        zz = z_back(k) if k <= NZ // 2 else z_on(k - NZ // 2)
        waits(tau.at[a_b, pl.ds(0, NX - 1)], bx_recv.at[k])
        push(a_b, zz, NZ + k)

    def a_z(h):
        up, down = z_back(h), z_on(h)
        if h == 0:
            waits(tau.at[a_a, pl.ds(0, NX - 1)], ax_recv.at[0])
            go(remote(bundle(a_a, z), bundle(a_a, z), az_send.at[0, 0], az_recv.at[0, 0], at_z(z_on(1))))
            go(remote(bundle(a_a, z), bundle(a_a, z), az_send.at[1, 0], az_recv.at[1, 0], at_z(z_back(1))))
            push(a_a, z, 0)
        elif h < NZ // 2:
            waits(bundle(a_a, up), az_recv.at[0, h - 1])
            waits(bundle(a_a, down), az_recv.at[1, h - 1])
            if h + 1 == NZ // 2:
                ref_u, ref_d = half_bundle(a_a, up, 0), half_bundle(a_a, down, 1)
            else:
                ref_u, ref_d = bundle(a_a, up), bundle(a_a, down)
            go(remote(ref_u, ref_u, az_send.at[0, h], az_recv.at[0, h], at_z(z_on(1))))
            go(remote(ref_d, ref_d, az_send.at[1, h], az_recv.at[1, h], at_z(z_back(1))))
            push(a_a, up, h)
            push(a_a, down, NZ // 2 + h)
        else:
            waits(half_bundle(a_a, up, 0), az_recv.at[0, h - 1])
            waits(half_bundle(a_a, up, 1), az_recv.at[1, h - 1])
            push(a_a, up, h)

    width = 512

    def gram(p, c):
        def body(b, _):
            cols = pl.ds(pl.multiple_of(b * width, width), width)
            r, i = vec[0, c, :, cols], vec[1, c, :, cols]
            co, si = trig[p, 0:1, cols], trig[p, 1:2, cols]
            wr = co * r + si * i
            wi = co * i - si * r
            for k, (lhs, rhs) in enumerate(((r, wr), (i, wi), (None, wr + wi))):
                if p == 0:
                    lh, ll = split(r - i if lhs is None else lhs)
                    left[k, 0, c, :, cols] = lh
                    left[k, 1, c, :, cols] = ll
                else:
                    lh, ll = left[k, 0, c, :, cols], left[k, 1, c, :, cols]
                rh, rl = split(rhs)
                acc[k] += dot(lh, rh) + dot(lh, rl) + dot(ll, rh)
            return 0

        lax.fori_loop(0, sites // width, body, 0)

    norm = 1.0 / math.sqrt(NC * sites * NSPACE * 2 * NY)

    def pair_copy(p):
        return remote(stage.at[p, 1 - core], pair_in.at[p], pair_send.at[p], pair_recv.at[p], partner)

    def finish_gram(p):
        p1, p2, p3 = acc[0], acc[1], acc[2]
        for ri, part in enumerate((p1 + p2, p3 - p1 + p2)):
            part = part * norm
            ebuf[ri, 0] = part[:, :128]
            ebuf[ri, 1] = part[:, 128:]
        for r in range(RANKS):
            for ri in range(2):
                for h in range(2):
                    lanes = pl.ds(h * 128, 128)
                    stage[p, r // PLANE, r % PLANE, ri, :, lanes] = ebuf[ri, h, pl.ds(r, 8, stride=32), :]
        go(pair_copy(p))

    def plane_stage(p):
        pair_copy(p).wait_recv()
        stage[p, core] += pair_in[p]

        def send(j, _):
            q = (place + j) % PLANE
            remote(
                stage.at[p, core, q], plane_in.at[p, place], plane_send.at[p], plane_recv.at[p],
                at_plane(core * PLANE + q),
            ).start()
            return 0

        lax.fori_loop(1, PLANE, send, 0)
        plane_in[p, place] = stage[p, core, place]

    def line_stage(p):
        waits(plane_in.at[p, pl.ds(0, PLANE - 1)], plane_recv.at[p])
        total = plane_in[p, 0]
        for q in range(1, PLANE):
            total = total + plane_in[p, q]
        line_in[p, z] = total

        def send(j, _):
            ref = line_in.at[p, z]
            remote(ref, ref, line_send.at[p], line_recv.at[p], at_z((z + j) % NZ)).start()
            return 0

        lax.fori_loop(1, NZ, send, 0)

    def full_stage(p):
        waits(line_in.at[p, pl.ds(0, NZ - 1)], line_recv.at[p])
        total = line_in[p, 0]
        for q in range(1, NZ):
            total = total + line_in[p, q]
        for ri in range(2):
            full[ri, p * 8 : p * 8 + 8, :] = total[ri]

    def pick_stage():
        def fill(d, _):
            sp, tl = at_plane(d)
            g = sp * (2 * NY) + tl
            u, v = graphs[g, 0], graphs[g, 1]
            for k, (block, ri) in enumerate(((u, 0), (u, 1), (v, 0), (v, 1))):
                pick[d, k : k + 1, :] = full[ri, pl.ds(block, 1), :]
            return 0

        lax.fori_loop(0, RANKS, fill, 0)

        def send(j, _):
            d = (rank + j) % RANKS
            remote(pick.at[d], picked.at[rank], pick_send.at[0], pick_recv.at[0], at_plane(d)).start()
            return 0

        lax.fori_loop(1, RANKS, send, 0)
        picked[rank] = pick[rank]

        def fill_rows(d, _):
            _, tl = at_plane(d)
            for k in range(4):
                rows[d, k : k + 1, :] = full[k % 2, pl.ds((k // 2) * 8 + tl, 1), :]
            return 0

        lax.fori_loop(0, RANKS, fill_rows, 0)

        def send_rows(j, _):
            d = (rank + j) % RANKS
            remote(rows.at[d], rowed.at[rank], rows_send.at[0], rows_recv.at[0], at_plane(d)).start()
            return 0

        lax.fori_loop(1, RANKS, send_rows, 0)
        rowed[rank] = rows[rank]

    def convert(a):
        def body(s, _):
            for ri in range(2):
                hi, lo = split(tau[a, s, ri])
                where = pl.ds(pl.multiple_of(s * 32, 32), 32)
                tau_hi[a, ri, where, :] = hi
                tau_lo[a, ri, where, :] = lo
            return 0

        lax.fori_loop(0, NSPACE, body, 0)

    def final():
        waits(picked.at[pl.ds(0, RANKS - 1)], pick_recv.at[0])
        u_re, u_im, v_re, v_im = (picked[:, k, :] for k in range(4))
        scale = 1.0 / math.sqrt(NEV)
        b_re = jnp.concatenate([u_re, u_im, v_re, v_im], axis=0) * scale
        b_im = jnp.concatenate([-u_im, u_re, -v_im, v_re], axis=0) * scale
        re_hi, re_lo = split(b_re)
        im_hi, im_lo = split(b_im)
        re_both = jnp.concatenate([re_hi, re_lo], axis=0)
        im_both = jnp.concatenate([im_hi, im_lo], axis=0)
        us, vs = [], []
        for a in range(SPIN):
            wide = dot(tau_hi[a, 0], re_both) + dot(tau_hi[a, 1], im_both)
            thin = dot(tau_lo[a, 0], re_hi) + dot(tau_lo[a, 1], im_hi)
            r = wide[:, :128] + wide[:, 128:] + thin
            us.append(r[:, :64])
            vs.append(r[:, 64:])
        u_all = jnp.concatenate(us, axis=1)
        v_all = jnp.concatenate(vs, axis=1)
        uh, ul = split(u_all)
        vh, vl = split(v_all)
        c4 = dot(uh, vh, TN) + dot(uh, vl, TN) + dot(ul, vh, TN)
        ii = lax.broadcasted_iota(jnp.int32, (128, NEV), 0)
        jj = lax.broadcasted_iota(jnp.int32, (128, NEV), 1)
        from_re = (jj == (ii % 4) * 64 + ii // 4).astype(F32)
        from_im = (jj == (ii % 4) * 64 + 32 + ii // 4).astype(F32)

        def exact(a, b, dims):
            return lax.dot_general(a, b, dims, precision=lax.Precision.HIGHEST, preferred_element_type=F32)

        nn = (((1,), (0,)), ((), ()))
        top = exact(from_re, c4, nn)
        low = exact(from_im, c4, nn)
        scale2 = 1.0 / math.sqrt(SPIN * NEV)
        out_ref[0] = (exact(top, from_re, NT) - exact(low, from_im, NT)) * scale2
        out_ref[1] = (exact(top, from_im, NT) + exact(low, from_re, NT)) * scale2

    def elementals():
        waits(rowed.at[pl.ds(0, RANKS - 1)], rows_recv.at[0])
        width8 = NEV // NSPACE
        for k in range(4):
            turned = pltpu.roll(rowed[:, k, :], (NEV - space * width8) % NEV, 1)
            el_ref[k // 2, k % 2] = turned[:, :width8]

    tau_first()
    acc[...] = jnp.zeros_like(acc)
    loads[0].wait()
    gram(0, 0)
    a_z(0)
    b_z(1)
    loads[1].wait()
    gram(0, 1)
    b_z(2)
    b_push(0)
    loads[2].wait()
    gram(0, 2)
    finish_gram(0)
    acc[...] = jnp.zeros_like(acc)
    b_z(3)
    gram(1, 0)
    plane_stage(0)
    a_z(1)
    b_push(1)
    b_push(5)
    gram(1, 1)
    b_z(4)
    gram(1, 2)
    finish_gram(1)
    line_stage(0)
    plane_stage(1)
    a_z(2)
    b_push(2)
    b_push(6)
    b_push(3)
    b_push(7)
    b_push(4)
    line_stage(1)
    full_stage(0)
    a_z(3)
    full_stage(1)
    a_z(4)
    pick_stage()
    for k in range(2 * NZ):
        waits(tau.at[0, pl.ds(0, NX)], push_recv.at[k])
    for a in range(SPIN):
        convert(a)
    final()
    elementals()
    for copy in started:
        copy.wait_send()
    for p in range(NMOM):
        waits(plane_in.at[p, pl.ds(0, PLANE - 1)], plane_send.at[p])
        waits(line_in.at[p, pl.ds(0, NZ - 1)], line_send.at[p])
    waits(picked.at[pl.ds(0, RANKS - 1)], pick_send.at[0])
    waits(rowed.at[pl.ds(0, RANKS - 1)], rows_send.at[0])


def per_device(eigenvectors, perambulator, momenta, graph_blocks):
    sites = eigenvectors.shape[3]
    eig = eigenvectors.transpose(0, 2, 1, 3)
    tau_in = perambulator.reshape(2, -1, NEV, SPIN).transpose(3, 0, 1, 2)
    sources = tau_in.shape[2]
    dma = pltpu.SemaphoreType.DMA
    el, out = pl.pallas_call(
        kernel,
        out_shape=(
            jax.ShapeDtypeStruct((NMOM, 2, 32, NEV // NSPACE), F32),
            jax.ShapeDtypeStruct((2, 128, 128), F32),
        ),
        in_specs=[
            pl.BlockSpec(memory_space=pltpu.SMEM),
            pl.BlockSpec(memory_space=pltpu.SMEM),
            pl.BlockSpec(memory_space=pl.ANY),
            pl.BlockSpec(memory_space=pltpu.VMEM),
        ],
        out_specs=(pl.BlockSpec(memory_space=pltpu.VMEM), pl.BlockSpec(memory_space=pltpu.VMEM)),
        scratch_shapes=[
            pltpu.VMEM((2, NC, NEV, sites), F32),
            pltpu.VMEM((3, 2, NC, NEV, sites), BF16),
            pltpu.VMEM((NMOM, 2, sites), F32),
            pltpu.VMEM((3, NEV, NEV), F32),
            pltpu.VMEM((2, 2, NEV, 128), F32),
            pltpu.VMEM((NMOM, 2, PLANE, 2, 8, NEV), F32),
            pltpu.VMEM((NMOM, PLANE, 2, 8, NEV), F32),
            pltpu.VMEM((NMOM, PLANE, 2, 8, NEV), F32),
            pltpu.VMEM((NMOM, NZ, 2, 8, NEV), F32),
            pltpu.VMEM((2, 16, NEV), F32),
            pltpu.VMEM((RANKS, 4, NEV), F32),
            pltpu.VMEM((RANKS, 4, NEV), F32),
            pltpu.VMEM((RANKS, 4, NEV), F32),
            pltpu.VMEM((RANKS, 4, NEV), F32),
            pltpu.VMEM((SPIN, NSPACE, 2, sources, NEV), F32),
            pltpu.VMEM((SPIN, 2, NSPACE * sources, NEV), BF16),
            pltpu.VMEM((SPIN, 2, NSPACE * sources, NEV), BF16),
            dma((NC,)),
            dma((2,)),
            dma((NMOM,)),
            dma((NMOM,)),
            dma((NMOM,)),
            dma((NMOM,)),
            dma((NMOM,)),
            dma((NMOM,)),
            dma((1,)),
            dma((1,)),
            dma((1,)),
            dma((1,)),
            dma((NX - 1,)),
            dma((1,)),
            dma((2, NZ // 2)),
            dma((2, NZ // 2)),
            dma((2, NZ // 2)),
            dma((2, NZ // 2)),
            dma((NZ, NX - 1)),
            dma((NZ,)),
            dma((2 * NZ,)),
            dma((2 * NZ,)),
        ],
        compiler_params=pltpu.CompilerParams(
            collective_id=0, has_side_effects=True, vmem_limit_bytes=60 * 2**20
        ),
    )(momenta, graph_blocks, eig, tau_in)
    return el, out[None]


def solution(mesh):
    return jax.shard_map(
        per_device,
        mesh=mesh,
        in_specs=(P(None, None, None, ("space", "tile")), P(None, "space", None), P(), P()),
        out_specs=(P(None, None, "tile", "space"), P(("space", "tile"), None, None, None)),
        check_vma=False,
    )
```

```python
import functools
import math

import jax
import jax.numpy as jnp
from jax import lax
from jax.experimental import pallas as pl
from jax.experimental.pallas import tpu as pltpu
from jax.sharding import PartitionSpec as P

NEV = 256
NC = 3
SPIN = 4
NMOM = 2
EDGE = 64
NX, NY, NZ = 4, 4, 8
PLANE = NX * NY
RANKS = 2 * PLANE
NSPACE = NX * NZ
BLOCK = 128
KDEV = 16
MESH = pl.DeviceIdType.MESH
F32 = jnp.float32
BF16 = jnp.bfloat16
NT = (((1,), (1,)), ((), ()))
TN = (((0,), (0,)), ((), ()))


def split(v):
    hi = v.astype(BF16)
    return hi, (v - hi.astype(F32)).astype(BF16)


def dot(a, b, dims=NT):
    return lax.dot_general(a, b, dims, preferred_element_type=F32)


def kernel(
    momenta_in, graphs_in, eig, sources_in, el_out, own_out, other_out,
    momenta, graphs, sources, el_ref, own_ref, vec, left, trig, acc, ebuf, stage, pair_in, plane_in, line_in, full, pick, picked, rows, rowed,
    tau_in, tau, tau_hi, tau_lo, foreign,
    load_sem, own_sem, pair_send, pair_recv, plane_send, plane_recv, line_send, line_recv,
    pick_send, pick_recv, rows_send, rows_recv,
    ax_send, ax_recv, az_send, az_recv, bz_send, bz_recv, bx_send, bx_recv, push_send, push_recv, swap_send, swap_recv, small_sem, out_sem,
):
    space, tile = lax.axis_index("space"), lax.axis_index("tile")
    x, z = space // NZ, space % NZ
    y, core = tile // 2, tile % 2
    place = x * NY + y
    rank = core * PLANE + place
    me = space * (2 * NY) + tile
    sites = vec.shape[3]

    def at_plane(other_rank):
        c, q = other_rank // PLANE, other_rank % PLANE
        return ((q // NY) * NZ + z, (q % NY) * 2 + c)

    def at_z(zz):
        return (x * NZ + zz, tile)

    def at_x(xx):
        return (xx * NZ + z, tile)

    partner = (space, y * 2 + 1 - core)

    def remote(src, dst, send, recv, device):
        return pltpu.make_async_remote_copy(
            src_ref=src, dst_ref=dst, send_sem=send, recv_sem=recv, device_id=device, device_id_type=MESH
        )

    small = [
        pltpu.make_async_copy(momenta_in, momenta, small_sem.at[0]),
        pltpu.make_async_copy(sources_in, sources, small_sem.at[1]),
        pltpu.make_async_copy(graphs_in, graphs, small_sem.at[2]),
    ]
    for copy in small:
        copy.start()
    loads = [pltpu.make_async_copy(eig.at[:, c], vec.at[:, c], load_sem.at[c]) for c in range(NC)]
    for load in loads:
        load.start()

    barrier = pltpu.get_barrier_semaphore()

    for j in range(1, RANKS):
        pl.semaphore_signal(barrier, inc=1, device_id=at_plane((rank + j) % RANKS), device_id_type=MESH)
    for j in range(1, NZ):
        pl.semaphore_signal(barrier, inc=1, device_id=at_z((z + j) % NZ), device_id_type=MESH)

    a_a, a_b = 2 * core, 2 * core + 1
    slot = z * NX + x

    def phases():
        site = me * sites + 128 * lax.broadcasted_iota(jnp.int32, (8, 128), 0)
        site = site + lax.broadcasted_iota(jnp.int32, (8, 128), 1)
        px, py, pz = site & (EDGE - 1), (site >> 6) & (EDGE - 1), site >> 12
        for p in range(NMOM):
            wave = (momenta[p, 0] * px + momenta[p, 1] * py + momenta[p, 2] * pz) & (EDGE - 1)
            angle = wave.astype(F32) * (2.0 * math.pi / EDGE)
            for k, value in enumerate((jnp.cos(angle), jnp.sin(angle))):
                for row in range(8):
                    trig[p, k : k + 1, row * 128 : row * 128 + 128] = value[row : row + 1, :]

    def spread():
        half = SPIN * 128
        jj = lax.broadcasted_iota(jnp.int32, (half, half), 0)
        col = lax.broadcasted_iota(jnp.int32, (half, half), 1)
        ones = (((jj & 3) * 128 + (jj >> 2)) == col).astype(F32).astype(BF16)
        first = pl.multiple_of((y % 2) * KDEV, KDEV)
        for h in range(2):
            lanes = slice(h * half, (h + 1) * half)
            value = jnp.concatenate([sources[0, pl.ds(first, KDEV), lanes], sources[1, pl.ds(first, KDEV), lanes]], axis=0)
            hi = value.astype(BF16)
            rest = value - hi.astype(F32)
            mid = rest.astype(BF16)
            low = (rest - mid.astype(F32)).astype(BF16)
            nn = (((1,), (0,)), ((), ()))
            parts = dot(jnp.concatenate([hi, mid, low], axis=0), ones, nn)
            n = 2 * KDEV
            moved = parts[:n] + parts[n : 2 * n] + parts[2 * n :]
            for a in range(SPIN):
                for ri in range(2):
                    tau_in[a, ri, :, h * 128 : h * 128 + 128] = moved[
                        ri * KDEV : (ri + 1) * KDEV, a * 128 : a * 128 + 128
                    ]

    started = []

    def go(copy):
        copy.start()
        started.append(copy)

    def bundle(a, zz):
        return tau.at[a, pl.ds(zz * NX, NX)]

    def half_bundle(a, zz, h):
        return tau.at[a, pl.ds(zz * NX + h * (NX // 2), NX // 2)]

    def push(a, zz, k):
        go(remote(bundle(a, zz), bundle(a, zz), push_send.at[k], push_recv.at[k], partner))

    def waits(ref, sem):
        pltpu.make_async_copy(ref, ref, sem).wait()

    def b_along_x(zz, k):
        for j in range(1, NX):
            ref = tau.at[a_b, zz * NX + x]
            go(remote(ref, ref, bx_send.at[k, j - 1], bx_recv.at[k], at_x((x + j) % NX)))

    def z_back(h):
        return (z + NZ - h) % NZ

    def z_on(h):
        return (z + h) % NZ

    def tau_first():
        own = [
            pltpu.make_async_copy(tau_in.at[a_a], tau.at[a_a, slot], own_sem.at[0]),
            pltpu.make_async_copy(tau_in.at[a_b], tau.at[a_b, slot], own_sem.at[1]),
        ]
        for copy in own:
            copy.start()
        for copy in own:
            copy.wait()
        for j in range(1, NX):
            ref = tau.at[a_a, slot]
            go(remote(ref, ref, ax_send.at[j - 1], ax_recv.at[0], at_x((x + j) % NX)))
        ref = tau.at[a_b, slot]
        go(remote(ref, ref, bz_send.at[0, 0], bz_recv.at[0, 0], at_z(z_on(1))))
        go(remote(ref, ref, bz_send.at[1, 0], bz_recv.at[1, 0], at_z(z_back(1))))

    def b_z(h):
        up, down = z_back(h), z_on(h)
        ref_up, ref_down = tau.at[a_b, up * NX + x], tau.at[a_b, down * NX + x]
        if h < NZ // 2:
            waits(ref_up, bz_recv.at[0, h - 1])
            waits(ref_down, bz_recv.at[1, h - 1])
            if h + 1 == NZ // 2:
                ref_u, ref_d = ref_up.at[0], ref_down.at[1]
            else:
                ref_u, ref_d = ref_up, ref_down
            go(remote(ref_u, ref_u, bz_send.at[0, h], bz_recv.at[0, h], at_z(z_on(1))))
            go(remote(ref_d, ref_d, bz_send.at[1, h], bz_recv.at[1, h], at_z(z_back(1))))
            b_along_x(up, h)
            b_along_x(down, NZ // 2 + h)
        else:
            waits(ref_up.at[0], bz_recv.at[0, h - 1])
            waits(ref_up.at[1], bz_recv.at[1, h - 1])
            b_along_x(up, h)

    def b_push(k):
        zz = z_back(k) if k <= NZ // 2 else z_on(k - NZ // 2)
        waits(tau.at[a_b, pl.ds(0, NX - 1)], bx_recv.at[k])
        push(a_b, zz, NZ + k)

    def a_z(h):
        up, down = z_back(h), z_on(h)
        if h == 0:
            waits(tau.at[a_a, pl.ds(0, NX - 1)], ax_recv.at[0])
            go(remote(bundle(a_a, z), bundle(a_a, z), az_send.at[0, 0], az_recv.at[0, 0], at_z(z_on(1))))
            go(remote(bundle(a_a, z), bundle(a_a, z), az_send.at[1, 0], az_recv.at[1, 0], at_z(z_back(1))))
            push(a_a, z, 0)
        elif h < NZ // 2:
            waits(bundle(a_a, up), az_recv.at[0, h - 1])
            waits(bundle(a_a, down), az_recv.at[1, h - 1])
            if h + 1 == NZ // 2:
                ref_u, ref_d = half_bundle(a_a, up, 0), half_bundle(a_a, down, 1)
            else:
                ref_u, ref_d = bundle(a_a, up), bundle(a_a, down)
            go(remote(ref_u, ref_u, az_send.at[0, h], az_recv.at[0, h], at_z(z_on(1))))
            go(remote(ref_d, ref_d, az_send.at[1, h], az_recv.at[1, h], at_z(z_back(1))))
            push(a_a, up, h)
            push(a_a, down, NZ // 2 + h)
        else:
            waits(half_bundle(a_a, up, 0), az_recv.at[0, h - 1])
            waits(half_bundle(a_a, up, 1), az_recv.at[1, h - 1])
            push(a_a, up, h)

    width = 512

    def gram(p, step):
        c, b = step // 2, step % 2
        cols = slice(b * width, (b + 1) * width)
        r, i = vec[0, c, :, cols], vec[1, c, :, cols]
        co, si = trig[p, 0:1, cols], trig[p, 1:2, cols]
        wr = co * r + si * i
        wi = co * i - si * r
        for k, (lhs, rhs) in enumerate(((r, wr), (i, wi), (None, wr + wi))):
            if p == 0:
                lh, ll = split(r - i if lhs is None else lhs)
                left[k, c, :NEV, cols] = lh
                left[k, c, NEV:, cols] = ll
            else:
                lh, ll = left[k, c, :NEV, cols], left[k, c, NEV:, cols]
            rh, rl = split(rhs)
            new = dot(lh, rh) + dot(lh, rl) + dot(ll, rh)
            if step == 0:
                acc[k] = new
            else:
                acc[k] += new

    def pair_copy(p):
        return remote(stage.at[p, 1 - core], pair_in.at[p], pair_send.at[p], pair_recv.at[p], partner)

    def finish_gram(p):
        p1, p2, p3 = acc[0], acc[1], acc[2]
        for ri, part in enumerate((p1 + p2, p3 - p1 + p2)):
            ebuf[ri, 0] = part[:, :128]
            ebuf[ri, 1] = part[:, 128:]
        for r in range(RANKS):
            for ri in range(2):
                for h in range(2):
                    lanes = pl.ds(h * 128, 128)
                    stage[p, r // PLANE, r % PLANE, ri, :, lanes] = ebuf[ri, h, pl.ds(r, 8, stride=32), :]
        go(pair_copy(p))

    def plane_stage(p):
        pair_copy(p).wait_recv()
        stage[p, core] += pair_in[p]

        def send(j, _):
            q = (place + j) % PLANE
            remote(
                stage.at[p, core, q], plane_in.at[p, place], plane_send.at[p], plane_recv.at[p],
                at_plane(core * PLANE + q),
            ).start()
            return 0

        lax.fori_loop(1, PLANE, send, 0)
        plane_in[p, place] = stage[p, core, place]

    def line_stage(p):
        waits(plane_in.at[p, pl.ds(0, PLANE - 1)], plane_recv.at[p])
        total = plane_in[p, 0]
        for q in range(1, PLANE):
            total = total + plane_in[p, q]
        line_in[p, z] = total

        def send(j, _):
            ref = line_in.at[p, z]
            remote(ref, ref, line_send.at[p], line_recv.at[p], at_z((z + j) % NZ)).start()
            return 0

        lax.fori_loop(1, NZ, send, 0)

    def full_stage(p):
        waits(line_in.at[p, pl.ds(0, NZ - 1)], line_recv.at[p])
        total = line_in[p, 0]
        for q in range(1, NZ):
            total = total + line_in[p, q]
        for ri in range(2):
            full[p * 8 : p * 8 + 8, ri, :] = total[ri]

    def pick_stage():
        def fill(d):
            sp, tl = at_plane(d)
            yy, cc = tl // 2, tl % 2
            for k, g in enumerate((sp * (2 * NY) + tl, sp * (2 * NY) + (yy + 1 - 2 * (yy % 2)) * 2 + cc)):
                for m in range(2):
                    first = k * 4 + m * 2
                    value = full[graphs[m, g]]
                    for h in range(2):
                        pick[d, h, first : first + 2, :] = value[:, h * 128 : h * 128 + 128]

        def send(j, _):
            d = (rank + j) % RANKS
            fill(d)
            remote(pick.at[d], picked.at[:, pl.ds(pl.multiple_of(rank * 8, 8), 8)], pick_send.at[0], pick_recv.at[0], at_plane(d)).start()
            return 0

        lax.fori_loop(1, RANKS, send, 0)
        fill(rank)
        for h in range(2):
            picked[h, pl.ds(pl.multiple_of(rank * 8, 8), 8), :] = pick[rank, h]

    def rows_stage():
        def send_rows(j, _):
            d = (rank + j) % RANKS
            _, tl = at_plane(d)
            rows[d, 0:2, :] = full[tl]
            rows[d, 2:4, :] = full[8 + tl]
            remote(rows.at[d], rowed.at[rank], rows_send.at[0], rows_recv.at[0], at_plane(d)).start()
            return 0

        lax.fori_loop(1, RANKS, send_rows, 0)
        rowed[rank, 0:2, :] = full[tile]
        rowed[rank, 2:4, :] = full[8 + tile]

    def convert(a):
        for s in range(NSPACE):
            for ri in range(2):
                hi, lo = split(tau[a, s, ri])
                tau_hi[a, ri, s * KDEV : (s + 1) * KDEV, :] = hi
                tau_lo[a, ri, s * KDEV : (s + 1) * KDEV, :] = lo

    norm = 1.0 / (NC * sites * NSPACE * 2 * NY)

    def moves(first_group):
        row = lax.broadcasted_iota(jnp.int32, (2 * BLOCK, 2 * BLOCK), 0)
        col = lax.broadcasted_iota(jnp.int32, (2 * BLOCK, 2 * BLOCK), 1)
        ri, a, i = row >> 7, row & 3, (row >> 2) & 31
        want = ri * BLOCK + ((a + first_group + ri) & 3) * 32 + i
        return (col == want).astype(F32).astype(BF16)

    def final():
        waits(picked.at[:, pl.ds(0, 8 * RANKS - 8)], pick_recv.at[0])
        pieces = []
        for k in range(2):
            u_re, u_im, v_re, v_im = (
                jnp.concatenate([picked[h, pl.ds(4 * k + m, RANKS, stride=8), :] for h in range(2)], axis=1)
                for m in range(4)
            )
            by_re = [split(v) for v in (u_re, u_im, v_re, v_im)]
            by_im = [split(v) for v in (-u_im, u_re, -v_im, v_re)]
            pieces.append((by_re, by_im))

        def weights(ri, part, a):
            return jnp.concatenate(
                [pieces[k][ri][(j - a) % 4][part] for k in range(2) for j in range(4)], axis=0
            )

        lane = lax.broadcasted_iota(jnp.int32, (1, 2 * BLOCK), 1)
        place_of = (lane >> 5) & 3
        groups = [None] * 4
        for a in range(SPIN):
            total = None
            for ri in range(2):
                w_hi, w_lo = weights(ri, 0, a), weights(ri, 1, a)
                hi, lo = tau_hi[a, ri], tau_lo[a, ri]
                new = dot(hi, w_hi) + dot(hi, w_lo) + dot(lo, w_hi)
                total = new if total is None else total + new
            for g in range(4):
                if groups[g] is None:
                    groups[g] = total
                else:
                    groups[g] = jnp.where(place_of == (a + g) % 4, total, groups[g])
        row_moves, col_moves = moves(0), moves(2)
        scale = norm / (NEV * math.sqrt(SPIN * NEV))
        nn = (((1,), (0,)), ((), ()))
        for k in (1, 0):
            lanes = slice(k * BLOCK, (k + 1) * BLOCK)
            uh, ul = split(jnp.concatenate([groups[0][:, lanes], groups[1][:, lanes]], axis=1))
            vh, vl = split(jnp.concatenate([groups[2][:, lanes], groups[3][:, lanes]], axis=1))
            c4 = dot(uh, vh, TN) + dot(uh, vl, TN) + dot(ul, vh, TN)
            hi, lo = split(c4 * scale)
            hi, lo = split(dot(row_moves, hi, nn) + dot(row_moves, lo, nn))
            c4 = dot(hi, col_moves) + dot(lo, col_moves)
            target = foreign if k == 1 else own_ref
            target[0] = c4[:BLOCK, :BLOCK] - c4[BLOCK:, BLOCK:]
            target[1] = c4[:BLOCK, BLOCK:] + c4[BLOCK:, :BLOCK]
            if k == 1:
                go(swap)

    mate = (space, (y + 1 - 2 * (y % 2)) * 2 + core)
    swap = remote(foreign, other_out, swap_send.at[0], swap_recv.at[0], mate)

    def elementals():
        waits(rowed.at[pl.ds(0, RANKS - 1)], rows_recv.at[0])
        width8 = NEV // NSPACE
        col = lax.broadcasted_iota(jnp.int32, (width8, NEV), 0)
        lane = lax.broadcasted_iota(jnp.int32, (width8, NEV), 1)
        ones = (lane == space * width8 + col).astype(F32)
        for k in range(4):
            el_ref[k // 2, k % 2] = lax.dot_general(
                ones, rowed[:, k, :], NT, precision=lax.Precision.HIGHEST, preferred_element_type=F32
            )

    small[0].wait()
    phases()
    small[1].wait()
    spread()
    small[2].wait()
    loads[0].wait()
    gram(0, 0)
    pl.semaphore_wait(barrier, RANKS - 1 + NZ - 1)
    tau_first()
    gram(0, 1)
    loads[1].wait()
    gram(0, 2)
    gram(0, 3)
    b_along_x(z, 0)
    loads[2].wait()
    gram(0, 4)
    b_z(1)
    a_z(0)
    gram(0, 5)
    finish_gram(0)
    gram(1, 0)
    b_z(2)
    gram(1, 1)
    plane_stage(0)
    gram(1, 2)
    b_push(0)
    b_z(3)
    gram(1, 3)
    a_z(1)
    gram(1, 4)
    b_push(1)
    b_push(5)
    gram(1, 5)
    finish_gram(1)
    b_z(4)
    plane_stage(1)
    a_z(2)
    b_push(2)
    b_push(6)
    line_stage(0)
    b_push(3)
    b_push(7)
    b_push(4)
    a_z(3)
    line_stage(1)
    a_z(4)
    full_stage(0)
    for k in range(2 * NZ):
        waits(tau.at[0, pl.ds(0, NX)], push_recv.at[k])
    for a in range(SPIN):
        convert(a)
    full_stage(1)
    pick_stage()
    rows_stage()
    final()
    own_copy = pltpu.make_async_copy(own_ref, own_out, out_sem.at[0])
    own_copy.start()
    elementals()
    el_copy = pltpu.make_async_copy(el_ref, el_out, out_sem.at[1])
    el_copy.start()
    swap.wait_recv()
    own_copy.wait()
    el_copy.wait()
    for copy in started:
        copy.wait_send()
    for p in range(NMOM):
        waits(plane_in.at[p, pl.ds(0, PLANE - 1)], plane_send.at[p])
        waits(line_in.at[p, pl.ds(0, NZ - 1)], line_send.at[p])
    waits(picked.at[:, pl.ds(0, 8 * RANKS - 8)], pick_send.at[0])
    waits(rowed.at[pl.ds(0, RANKS - 1)], rows_send.at[0])


def per_device(eigenvectors, perambulator, momenta, graph_blocks):
    sites = eigenvectors.shape[3]
    eig = eigenvectors.transpose(0, 2, 1, 3)
    dma = pltpu.SemaphoreType.DMA
    width8 = NEV // NSPACE
    el, own, other = pl.pallas_call(
        kernel,
        out_shape=(
            jax.ShapeDtypeStruct((NMOM, 2, width8, 32), F32),
            jax.ShapeDtypeStruct((2, BLOCK, BLOCK), F32),
            jax.ShapeDtypeStruct((2, BLOCK, BLOCK), F32),
        ),
        in_specs=[
            pl.BlockSpec(memory_space=pl.ANY),
            pl.BlockSpec(memory_space=pl.ANY),
            pl.BlockSpec(memory_space=pl.ANY),
            pl.BlockSpec(memory_space=pl.ANY),
        ],
        out_specs=(pl.BlockSpec(memory_space=pl.ANY),) * 3,
        scratch_shapes=[
            pltpu.SMEM((NMOM, 3), jnp.int32),
            pltpu.SMEM((2, NSPACE * 2 * NY), jnp.int32),
            pltpu.VMEM((2, 2 * KDEV, SPIN * NEV), F32),
            pltpu.VMEM((NMOM, 2, width8, 32), F32),
            pltpu.VMEM((2, BLOCK, BLOCK), F32),
            pltpu.VMEM((2, NC, NEV, sites), F32),
            pltpu.VMEM((3, NC, 2 * NEV, sites), BF16),
            pltpu.VMEM((NMOM, 2, sites), F32),
            pltpu.VMEM((3, NEV, NEV), F32),
            pltpu.VMEM((2, 2, NEV, 128), F32),
            pltpu.VMEM((NMOM, 2, PLANE, 2, 8, NEV), F32),
            pltpu.VMEM((NMOM, PLANE, 2, 8, NEV), F32),
            pltpu.VMEM((NMOM, PLANE, 2, 8, NEV), F32),
            pltpu.VMEM((NMOM, NZ, 2, 8, NEV), F32),
            pltpu.VMEM((16, 2, NEV), F32),
            pltpu.VMEM((RANKS, 2, 8, 128), F32),
            pltpu.VMEM((2, RANKS * 8, 128), F32),
            pltpu.VMEM((RANKS, 4, NEV), F32),
            pltpu.VMEM((RANKS, 4, NEV), F32),
            pltpu.VMEM((SPIN, 2, KDEV, NEV), F32),
            pltpu.VMEM((SPIN, NSPACE, 2, KDEV, NEV), F32),
            pltpu.VMEM((SPIN, 2, NSPACE * KDEV, NEV), BF16),
            pltpu.VMEM((SPIN, 2, NSPACE * KDEV, NEV), BF16),
            pltpu.VMEM((2, BLOCK, BLOCK), F32),
            dma((NC,)),
            dma((2,)),
            dma((NMOM,)),
            dma((NMOM,)),
            dma((NMOM,)),
            dma((NMOM,)),
            dma((NMOM,)),
            dma((NMOM,)),
            dma((1,)),
            dma((1,)),
            dma((1,)),
            dma((1,)),
            dma((NX - 1,)),
            dma((1,)),
            dma((2, NZ // 2)),
            dma((2, NZ // 2)),
            dma((2, NZ // 2)),
            dma((2, NZ // 2)),
            dma((NZ, NX - 1)),
            dma((NZ,)),
            dma((2 * NZ,)),
            dma((2 * NZ,)),
            dma((1,)),
            dma((1,)),
            dma((3,)),
            dma((2,)),
        ],
        compiler_params=pltpu.CompilerParams(
            collective_id=0, has_side_effects=True, vmem_limit_bytes=60 * 2**20
        ),
    )(momenta, graph_blocks.T, eig, perambulator)
    norm = 1.0 / math.sqrt(NC * sites * NSPACE * 2 * NY)

    def finish(el_ref, own_ref, other_ref, el_out, sum_out):
        el_out[...] = el_ref[...] * norm
        sum_out[...] = own_ref[...] + other_ref[...]

    el, out = pl.pallas_call(
        finish,
        out_shape=(jax.ShapeDtypeStruct(el.shape, F32), jax.ShapeDtypeStruct(own.shape, F32)),
    )(el, own, other)
    return el.transpose(0, 1, 3, 2), out[None]


def solution(mesh):
    return jax.shard_map(
        per_device,
        mesh=mesh,
        in_specs=(P(None, None, None, ("space", "tile")), P(None, "space", None), P(), P()),
        out_specs=(P(None, None, "tile", "space"), P(("space", "tile"), None, None, None)),
        check_vma=False,
    )
```

```python
import functools
import math

import jax
import jax.numpy as jnp
from jax import lax
from jax.experimental import pallas as pl
from jax.experimental.pallas import tpu as pltpu
from jax.sharding import PartitionSpec as P

NEV = 256
NC = 3
SPIN = 4
NMOM = 2
EDGE = 64
NX, NY, NZ = 4, 4, 8
PLANE = NX * NY
RANKS = 2 * PLANE
NSPACE = NX * NZ
BLOCK = 128
KDEV = 16
MESH = pl.DeviceIdType.MESH
PLANE_FAR = tuple(
    sorted(
        ((dx, dy) for dx in range(NX) for dy in range(NY) if dx or dy),
        key=lambda d: -min(d[0], NX - d[0]) - min(d[1], NY - d[1]),
    )
)
F32 = jnp.float32
BF16 = jnp.bfloat16
NT = (((1,), (1,)), ((), ()))
TN = (((0,), (0,)), ((), ()))


def split(v):
    hi = v.astype(BF16)
    return hi, (v - hi.astype(F32)).astype(BF16)


def dot(a, b, dims=NT):
    return lax.dot_general(a, b, dims, preferred_element_type=F32)


def kernel(
    momenta_in, graphs_in, eig, sources_in, el_out, own_out, other_out,
    momenta, graphs, sources, el_ref, own_ref, vec, left, trig, acc, ebuf, stage, pair_in, plane_in, line_in, full, pick, picked, rows, rowed,
    tau_in, tau, tau_hi, tau_lo, wts, foreign,
    load_sem, own_sem, pair_send, pair_recv, plane_send, plane_recv, line_send, line_recv,
    pick_send, pick_recv, rows_send, rows_recv,
    ax_send, ax_recv, az_send, az_recv, bz_send, bz_recv, bx_send, bx_recv, push_send, push_recv, swap_send, swap_recv, small_sem, out_sem,
):
    space, tile = lax.axis_index("space"), lax.axis_index("tile")
    x, z = space // NZ, space % NZ
    y, core = tile // 2, tile % 2
    place = x * NY + y
    rank = core * PLANE + place
    me = space * (2 * NY) + tile
    sites = vec.shape[3]

    def at_plane(other_rank):
        c, q = other_rank // PLANE, other_rank % PLANE
        return ((q // NY) * NZ + z, (q % NY) * 2 + c)

    def at_z(zz):
        return (x * NZ + zz, tile)

    def at_x(xx):
        return (xx * NZ + z, tile)

    partner = (space, y * 2 + 1 - core)

    def remote(src, dst, send, recv, device):
        return pltpu.make_async_remote_copy(
            src_ref=src, dst_ref=dst, send_sem=send, recv_sem=recv, device_id=device, device_id_type=MESH
        )

    small = [
        pltpu.make_async_copy(momenta_in, momenta, small_sem.at[0]),
        pltpu.make_async_copy(sources_in, sources, small_sem.at[1]),
        pltpu.make_async_copy(graphs_in, graphs, small_sem.at[2]),
    ]
    for copy in small:
        copy.start()
    loads = [pltpu.make_async_copy(eig.at[:, c], vec.at[:, c], load_sem.at[c]) for c in range(NC)]
    for load in loads:
        load.start()

    barrier = pltpu.get_barrier_semaphore()

    for j in range(1, RANKS):
        pl.semaphore_signal(barrier, inc=1, device_id=at_plane((rank + j) % RANKS), device_id_type=MESH)
    for j in range(1, NZ):
        pl.semaphore_signal(barrier, inc=1, device_id=at_z((z + j) % NZ), device_id_type=MESH)

    a_a, a_b = 2 * core, 2 * core + 1
    slot = z * NX + x

    def phases():
        site = me * sites + 128 * lax.broadcasted_iota(jnp.int32, (8, 128), 0)
        site = site + lax.broadcasted_iota(jnp.int32, (8, 128), 1)
        px, py, pz = site & (EDGE - 1), (site >> 6) & (EDGE - 1), site >> 12
        for p in range(NMOM):
            wave = (momenta[p, 0] * px + momenta[p, 1] * py + momenta[p, 2] * pz) & (EDGE - 1)
            angle = wave.astype(F32) * (2.0 * math.pi / EDGE)
            for k, value in enumerate((jnp.cos(angle), jnp.sin(angle))):
                for row in range(8):
                    trig[p, k : k + 1, row * 128 : row * 128 + 128] = value[row : row + 1, :]

    def spread():
        half = SPIN * 128
        jj = lax.broadcasted_iota(jnp.int32, (half, half), 0)
        col = lax.broadcasted_iota(jnp.int32, (half, half), 1)
        ones = (((jj & 3) * 128 + (jj >> 2)) == col).astype(F32).astype(BF16)
        first = pl.multiple_of((y % 2) * KDEV, KDEV)
        for h in range(2):
            lanes = slice(h * half, (h + 1) * half)
            value = jnp.concatenate([sources[0, pl.ds(first, KDEV), lanes], sources[1, pl.ds(first, KDEV), lanes]], axis=0)
            hi = value.astype(BF16)
            rest = value - hi.astype(F32)
            mid = rest.astype(BF16)
            low = (rest - mid.astype(F32)).astype(BF16)
            nn = (((1,), (0,)), ((), ()))
            parts = dot(jnp.concatenate([hi, mid, low], axis=0), ones, nn)
            n = 2 * KDEV
            moved = parts[:n] + parts[n : 2 * n] + parts[2 * n :]
            for a in range(SPIN):
                for ri in range(2):
                    tau_in[a, ri, :, h * 128 : h * 128 + 128] = moved[
                        ri * KDEV : (ri + 1) * KDEV, a * 128 : a * 128 + 128
                    ]

    def go(copy):
        copy.start()

    def bundle(a, zz):
        return tau.at[a, pl.ds(zz * NX, NX)]

    def half_bundle(a, zz, h):
        return tau.at[a, pl.ds(zz * NX + h * (NX // 2), NX // 2)]

    def push(a, zz, k):
        go(remote(bundle(a, zz), bundle(a, zz), push_send.at[0], push_recv.at[0], partner))

    def waits(ref, sem):
        pltpu.make_async_copy(ref, ref, sem).wait()

    def b_along_x(zz, k):
        for j in range(1, NX):
            ref = tau.at[a_b, zz * NX + x]
            go(remote(ref, ref, bx_send.at[0], bx_recv.at[k], at_x((x + j) % NX)))

    def z_back(h):
        return (z + NZ - h) % NZ

    def z_on(h):
        return (z + h) % NZ

    def tau_first():
        own = [
            pltpu.make_async_copy(tau_in.at[a_a], tau.at[a_a, slot], own_sem.at[0]),
            pltpu.make_async_copy(tau_in.at[a_b], tau.at[a_b, slot], own_sem.at[1]),
        ]
        for copy in own:
            copy.start()
        for copy in own:
            copy.wait()
        for j in range(1, NX):
            ref = tau.at[a_a, slot]
            go(remote(ref, ref, ax_send.at[0], ax_recv.at[0], at_x((x + j) % NX)))
        ref = tau.at[a_b, slot]
        go(remote(ref, ref, bz_send.at[0], bz_recv.at[0, 0], at_z(z_on(1))))
        go(remote(ref, ref, bz_send.at[0], bz_recv.at[1, 0], at_z(z_back(1))))

    def b_z(h):
        up, down = z_back(h), z_on(h)
        ref_up, ref_down = tau.at[a_b, up * NX + x], tau.at[a_b, down * NX + x]
        if h < NZ // 2:
            waits(ref_up, bz_recv.at[0, h - 1])
            waits(ref_down, bz_recv.at[1, h - 1])
            if h + 1 == NZ // 2:
                ref_u, ref_d = ref_up.at[0], ref_down.at[1]
            else:
                ref_u, ref_d = ref_up, ref_down
            go(remote(ref_u, ref_u, bz_send.at[0], bz_recv.at[0, h], at_z(z_on(1))))
            go(remote(ref_d, ref_d, bz_send.at[0], bz_recv.at[1, h], at_z(z_back(1))))
            b_along_x(up, h)
            b_along_x(down, NZ // 2 + h)
        else:
            waits(ref_up.at[0], bz_recv.at[0, h - 1])
            waits(ref_up.at[1], bz_recv.at[1, h - 1])
            b_along_x(up, h)

    def b_push(k):
        zz = z_back(k) if k <= NZ // 2 else z_on(k - NZ // 2)
        waits(tau.at[a_b, pl.ds(0, NX - 1)], bx_recv.at[k])
        push(a_b, zz, NZ + k)

    def a_z(h, part):
        up, down = z_back(h), z_on(h)

        def onward(ref, way):
            to = at_z(z_on(1)) if way == 0 else at_z(z_back(1))
            go(remote(ref, ref, az_send.at[0], az_recv.at[way, h, part], to))

        def push_half(zz, k):
            ref = half_bundle(a_a, zz, part)
            go(remote(ref, ref, push_send.at[0], push_recv.at[0], partner))

        if h == 0:
            if part == 0:
                waits(tau.at[a_a, pl.ds(0, NX - 1)], ax_recv.at[0])
            onward(half_bundle(a_a, z, part), 0)
            onward(half_bundle(a_a, z, part), 1)
            push_half(z, 0)
        elif h < NZ // 2:
            waits(half_bundle(a_a, up, part), az_recv.at[0, h - 1, part])
            waits(half_bundle(a_a, down, part), az_recv.at[1, h - 1, part])
            if h + 1 < NZ // 2 or part == 0:
                onward(half_bundle(a_a, up, part), 0)
            if h + 1 < NZ // 2 or part == 1:
                onward(half_bundle(a_a, down, part), 1)
            push_half(up, h)
            push_half(down, NZ // 2 + h)
        else:
            waits(half_bundle(a_a, up, part), az_recv.at[part, h - 1, part])
            push_half(up, h)

    zero = space // NSPACE

    def gram(p, c):
        def body(c, _):
            r, i = vec[0, c], vec[1, c]
            co, si = trig[p, 0:1, :], trig[p, 1:2, :]
            wr = co * r + si * i
            wi = co * i - si * r
            for k, (lhs, rhs) in enumerate(((r, wr), (i, wi), (None, wr + wi))):
                if p == 0:
                    lh, ll = split(r - i if lhs is None else lhs)
                    left[k, c, :NEV] = lh
                    left[k, c, NEV:] = ll
                else:
                    lh, ll = left[k, c, :NEV], left[k, c, NEV:]
                rh, rl = split(rhs)
                wide = dot(jnp.concatenate([lh, ll], axis=0), rh)
                acc[k] += wide[:NEV] + wide[NEV:] + dot(lh, rl)
            return 0

        lax.fori_loop(zero + c, zero + c + 1, body, 0)

    def pair_copy(p):
        return remote(stage.at[p, 1 - core], pair_in.at[p], pair_send.at[p], pair_recv.at[p], partner)

    def finish_gram(p):
        p1, p2, p3 = acc[0], acc[1], acc[2]
        for ri, part in enumerate((p1 + p2, p3 - p1 + p2)):
            ebuf[ri, 0] = part[:, :128]
            ebuf[ri, 1] = part[:, 128:]
        for r in range(RANKS):
            for ri in range(2):
                for h in range(2):
                    lanes = pl.ds(h * 128, 128)
                    stage[p, r // PLANE, r % PLANE, ri, :, lanes] = ebuf[ri, h, pl.ds(r, 8, stride=32), :]
        go(pair_copy(p))

    def plane_stage(p):
        pair_copy(p).wait_recv()
        stage[p, core] += pair_in[p]

        for dx, dy in PLANE_FAR:
            q = ((x + dx) % NX) * NY + (y + dy) % NY
            remote(
                stage.at[p, core, q], plane_in.at[p, place], plane_send.at[p], plane_recv.at[p],
                at_plane(core * PLANE + q),
            ).start()
        plane_in[p, place] = stage[p, core, place]

    def line_stage(p):
        waits(plane_in.at[p, pl.ds(0, PLANE - 1)], plane_recv.at[p])
        total = plane_in[p, 0]
        for q in range(1, PLANE):
            total = total + plane_in[p, q]
        line_in[p, z] = total

        for dz in (4, 3, 5, 2, 6, 1, 7):
            ref = line_in.at[p, z]
            remote(ref, ref, line_send.at[p], line_recv.at[p], at_z((z + dz) % NZ)).start()

    def full_stage(p):
        waits(line_in.at[p, pl.ds(0, NZ - 1)], line_recv.at[p])
        total = line_in[p, 0]
        for q in range(1, NZ):
            total = total + line_in[p, q]
        for ri in range(2):
            full[p * 8 : p * 8 + 8, ri, :] = total[ri]

    def pick_stage():
        def fill(d):
            sp, tl = at_plane(d)
            yy, cc = tl // 2, tl % 2
            for k, g in enumerate((sp * (2 * NY) + tl, sp * (2 * NY) + (yy + 1 - 2 * (yy % 2)) * 2 + cc)):
                for m in range(2):
                    first = k * 4 + m * 2
                    value = full[graphs[m, g]]
                    for h in range(2):
                        pick[d, h, first : first + 2, :] = value[:, h * 128 : h * 128 + 128]

        for dx, dy in PLANE_FAR + ((0, 0),):
            for cc in (core, 1 - core):
                if (dx, dy) == (0, 0) and cc is core:
                    continue
                d = cc * PLANE + ((x + dx) % NX) * NY + (y + dy) % NY
                fill(d)
                remote(pick.at[d], picked.at[:, pl.ds(pl.multiple_of(rank * 8, 8), 8)], pick_send.at[0], pick_recv.at[0], at_plane(d)).start()

        fill(rank)
        for h in range(2):
            picked[h, pl.ds(pl.multiple_of(rank * 8, 8), 8), :] = pick[rank, h]

    def rows_stage():
        def send_rows(j, _):
            d = (rank + j) % RANKS
            _, tl = at_plane(d)
            rows[d, 0:2, :] = full[tl]
            rows[d, 2:4, :] = full[8 + tl]
            remote(rows.at[d], rowed.at[rank], rows_send.at[0], rows_recv.at[0], at_plane(d)).start()
            return 0

        lax.fori_loop(1, RANKS, send_rows, 0)
        rowed[rank, 0:2, :] = full[tile]
        rowed[rank, 2:4, :] = full[8 + tile]

    def convert(a):
        for s in range(NSPACE):
            for ri in range(2):
                hi, lo = split(tau[a, s, ri])
                tau_hi[a, ri, s * KDEV : (s + 1) * KDEV, :] = hi
                tau_lo[a, ri, s * KDEV : (s + 1) * KDEV, :] = lo

    norm = 1.0 / (NC * sites * NSPACE * 2 * NY)

    def moves(first_group):
        row = lax.broadcasted_iota(jnp.int32, (2 * BLOCK, 2 * BLOCK), 0)
        col = lax.broadcasted_iota(jnp.int32, (2 * BLOCK, 2 * BLOCK), 1)
        ri, a, i = row >> 7, row & 3, (row >> 2) & 31
        want = ri * BLOCK + ((a + first_group + ri) & 3) * 32 + i
        return (col == want).astype(F32).astype(BF16)

    def final():
        waits(picked.at[:, pl.ds(0, 8 * RANKS - 8)], pick_recv.at[0])
        for k in range(2):
            u_re, u_im, v_re, v_im = (
                jnp.concatenate([picked[h, pl.ds(4 * k + m, RANKS, stride=8), :] for h in range(2)], axis=1)
                for m in range(4)
            )
            for ri, values in enumerate(((u_re, u_im, v_re, v_im), (-u_im, u_re, -v_im, v_re))):
                for j, value in enumerate(values):
                    for part, half in enumerate(split(value)):
                        wts[ri, part, k, j * 32 : j * 32 + 32, :] = half
                        if j < 3:
                            wts[ri, part, k, j * 32 + BLOCK : j * 32 + BLOCK + 32, :] = half

        lane = lax.broadcasted_iota(jnp.int32, (1, BLOCK), 1)
        place_of = lane >> 5
        row_moves, col_moves = moves(0), moves(2)
        scale = norm / (NEV * math.sqrt(SPIN * NEV))
        nn = (((1,), (0,)), ((), ()))
        for k in (1, 0):
            groups = [None] * 4
            for a in range(SPIN):
                first = (-a % 4) * 32
                total = None
                for ri in range(2):
                    w_hi = wts[ri, 0, k, first : first + BLOCK, :]
                    both = jnp.concatenate([w_hi, wts[ri, 1, k, first : first + BLOCK, :]], axis=0)
                    wide = dot(tau_hi[a, ri], both)
                    new = wide[:, :BLOCK] + wide[:, BLOCK:] + dot(tau_lo[a, ri], w_hi)
                    total = new if total is None else total + new
                for g in range(4):
                    if groups[g] is None:
                        groups[g] = total
                    else:
                        groups[g] = jnp.where(place_of == (a + g) % 4, total, groups[g])
            uh, ul = split(jnp.concatenate([groups[0], groups[1]], axis=1))
            vh, vl = split(jnp.concatenate([groups[2], groups[3]], axis=1))
            c4 = dot(uh, vh, TN) + dot(uh, vl, TN) + dot(ul, vh, TN)
            hi, lo = split(c4 * scale)
            hi, lo = split(dot(row_moves, hi, nn) + dot(row_moves, lo, nn))
            c4 = dot(hi, col_moves) + dot(lo, col_moves)
            target = foreign if k == 1 else own_ref
            target[0] = c4[:BLOCK, :BLOCK] - c4[BLOCK:, BLOCK:]
            target[1] = c4[:BLOCK, BLOCK:] + c4[BLOCK:, :BLOCK]
            if k == 1:
                go(swap)

    mate = (space, (y + 1 - 2 * (y % 2)) * 2 + core)
    swap = remote(foreign, other_out, swap_send.at[0], swap_recv.at[0], mate)

    def elementals():
        waits(rowed.at[pl.ds(0, RANKS - 1)], rows_recv.at[0])
        width8 = NEV // NSPACE
        col = lax.broadcasted_iota(jnp.int32, (width8, NEV), 0)
        lane = lax.broadcasted_iota(jnp.int32, (width8, NEV), 1)
        ones = (lane == space * width8 + col).astype(F32)
        for k in range(4):
            el_ref[k // 2, k % 2] = lax.dot_general(
                ones, rowed[:, k, :], NT, precision=lax.Precision.HIGHEST, preferred_element_type=F32
            )

    acc[...] = jnp.zeros_like(acc)
    small[0].wait()
    phases()
    loads[0].wait()
    gram(0, 0)
    small[1].wait()
    spread()
    small[2].wait()
    pl.semaphore_wait(barrier, RANKS - 1 + NZ - 1)
    tau_first()
    loads[1].wait()
    gram(0, 1)
    b_along_x(z, 0)
    loads[2].wait()
    gram(0, 2)
    finish_gram(0)
    acc[...] = jnp.zeros_like(acc)
    b_z(1)
    a_z(0, 0)
    a_z(0, 1)
    gram(1, 0)
    plane_stage(0)
    gram(1, 1)
    b_z(2)
    a_z(1, 0)
    b_push(0)
    gram(1, 2)
    finish_gram(1)
    a_z(1, 1)
    plane_stage(1)
    b_z(3)
    a_z(2, 0)
    b_push(1)
    b_push(5)
    line_stage(0)
    a_z(2, 1)
    b_z(4)
    a_z(3, 0)
    b_push(2)
    b_push(6)
    line_stage(1)
    a_z(3, 1)
    b_push(3)
    b_push(7)
    b_push(4)
    full_stage(0)
    a_z(4, 0)
    full_stage(1)
    pick_stage()
    a_z(4, 1)
    rows_stage()
    waits(tau.at[pl.ds(0, 2)], push_recv.at[0])
    for a in range(SPIN):
        convert(a)
    final()
    own_copy = pltpu.make_async_copy(own_ref, own_out, out_sem.at[0])
    own_copy.start()
    elementals()
    el_copy = pltpu.make_async_copy(el_ref, el_out, out_sem.at[1])
    el_copy.start()
    swap.wait_recv()
    own_copy.wait()
    el_copy.wait()
    waits(tau.at[0, pl.ds(0, NX - 1)], ax_send.at[0])
    waits(tau.at[0, pl.ds(0, NX * (NZ - 1))], az_send.at[0])
    waits(tau.at[0, pl.ds(0, NZ - 1)], bz_send.at[0])
    waits(tau.at[0, pl.ds(0, NZ * (NX - 1))], bx_send.at[0])
    waits(tau.at[pl.ds(0, 2)], push_send.at[0])
    swap.wait_send()
    for p in range(NMOM):
        pair_copy(p).wait_send()
        waits(plane_in.at[p, pl.ds(0, PLANE - 1)], plane_send.at[p])
        waits(line_in.at[p, pl.ds(0, NZ - 1)], line_send.at[p])
    waits(picked.at[:, pl.ds(0, 8 * RANKS - 8)], pick_send.at[0])
    waits(rowed.at[pl.ds(0, RANKS - 1)], rows_send.at[0])


def per_device(eigenvectors, perambulator, momenta, graph_blocks):
    sites = eigenvectors.shape[3]
    eig = eigenvectors.transpose(0, 2, 1, 3)
    dma = pltpu.SemaphoreType.DMA
    width8 = NEV // NSPACE
    el, own, other = pl.pallas_call(
        kernel,
        out_shape=(
            jax.ShapeDtypeStruct((NMOM, 2, width8, 32), F32),
            jax.ShapeDtypeStruct((2, BLOCK, BLOCK), F32),
            jax.ShapeDtypeStruct((2, BLOCK, BLOCK), F32),
        ),
        in_specs=[
            pl.BlockSpec(memory_space=pltpu.HBM),
            pl.BlockSpec(memory_space=pltpu.HBM),
            pl.BlockSpec(memory_space=pltpu.HBM),
            pl.BlockSpec(memory_space=pltpu.HBM),
        ],
        out_specs=(pl.BlockSpec(memory_space=pl.ANY),) * 3,
        scratch_shapes=[
            pltpu.SMEM((NMOM, 3), jnp.int32),
            pltpu.SMEM((2, NSPACE * 2 * NY), jnp.int32),
            pltpu.VMEM((2, 2 * KDEV, SPIN * NEV), F32),
            pltpu.VMEM((NMOM, 2, width8, 32), F32),
            pltpu.VMEM((2, BLOCK, BLOCK), F32),
            pltpu.VMEM((2, NC, NEV, sites), F32),
            pltpu.VMEM((3, NC, 2 * NEV, sites), BF16),
            pltpu.VMEM((NMOM, 2, sites), F32),
            pltpu.VMEM((3, NEV, NEV), F32),
            pltpu.VMEM((2, 2, NEV, 128), F32),
            pltpu.VMEM((NMOM, 2, PLANE, 2, 8, NEV), F32),
            pltpu.VMEM((NMOM, PLANE, 2, 8, NEV), F32),
            pltpu.VMEM((NMOM, PLANE, 2, 8, NEV), F32),
            pltpu.VMEM((NMOM, NZ, 2, 8, NEV), F32),
            pltpu.VMEM((16, 2, NEV), F32),
            pltpu.VMEM((RANKS, 2, 8, 128), F32),
            pltpu.VMEM((2, RANKS * 8, 128), F32),
            pltpu.VMEM((RANKS, 4, NEV), F32),
            pltpu.VMEM((RANKS, 4, NEV), F32),
            pltpu.VMEM((SPIN, 2, KDEV, NEV), F32),
            pltpu.VMEM((SPIN, NSPACE, 2, KDEV, NEV), F32),
            pltpu.VMEM((SPIN, 2, NSPACE * KDEV, NEV), BF16),
            pltpu.VMEM((SPIN, 2, NSPACE * KDEV, NEV), BF16),
            pltpu.VMEM((2, 2, 2, 7 * 32, NEV), BF16),
            pltpu.VMEM((2, BLOCK, BLOCK), F32),
            dma((NC,)),
            dma((2,)),
            dma((NMOM,)),
            dma((NMOM,)),
            dma((NMOM,)),
            dma((NMOM,)),
            dma((NMOM,)),
            dma((NMOM,)),
            dma((1,)),
            dma((1,)),
            dma((1,)),
            dma((1,)),
            dma((1,)),
            dma((1,)),
            dma((1,)),
            dma((2, NZ // 2, 2)),
            dma((1,)),
            dma((2, NZ // 2)),
            dma((1,)),
            dma((NZ,)),
            dma((1,)),
            dma((1,)),
            dma((1,)),
            dma((1,)),
            dma((3,)),
            dma((2,)),
        ],
        compiler_params=pltpu.CompilerParams(
            collective_id=0, has_side_effects=True, vmem_limit_bytes=48 * 2**20
        ),
    )(*(pltpu.with_memory_space_constraint(v, pltpu.HBM) for v in (momenta, graph_blocks.T, eig, perambulator)))
    norm = 1.0 / math.sqrt(NC * sites * NSPACE * 2 * NY)

    def finish(el_ref, own_ref, other_ref, el_out, sum_out, el_buf, own_buf, other_buf, sems):
        pairs = ((own_ref, own_buf), (other_ref, other_buf), (el_ref, el_buf))
        copies = [pltpu.make_async_copy(a, b, sems.at[k]) for k, (a, b) in enumerate(pairs)]
        for copy in copies:
            copy.start()
        copies[0].wait()
        copies[1].wait()
        own_buf[...] += other_buf[...]
        sum_copy = pltpu.make_async_copy(own_buf, sum_out, sems.at[3])
        sum_copy.start()
        copies[2].wait()
        el_buf[...] *= norm
        el_copy = pltpu.make_async_copy(el_buf, el_out, sems.at[4])
        el_copy.start()
        sum_copy.wait()
        el_copy.wait()

    anywhere = pl.BlockSpec(memory_space=pl.ANY)
    hbm = pl.BlockSpec(memory_space=pltpu.HBM)
    el, out = pl.pallas_call(
        finish,
        out_shape=(jax.ShapeDtypeStruct(el.shape, F32), jax.ShapeDtypeStruct(own.shape, F32)),
        in_specs=[anywhere] * 3,
        out_specs=(hbm, hbm),
        scratch_shapes=[
            pltpu.VMEM(el.shape, F32),
            pltpu.VMEM(own.shape, F32),
            pltpu.VMEM(own.shape, F32),
            dma((5,)),
        ],
        compiler_params=pltpu.CompilerParams(vmem_limit_bytes=8 * 2**20),
    )(el, own, other)
    return el.transpose(0, 1, 3, 2), out[None]


def solution(mesh):
    return jax.shard_map(
        per_device,
        mesh=mesh,
        in_specs=(P(None, None, None, ("space", "tile")), P(None, "space", None), P(), P()),
        out_specs=(P(None, None, "tile", "space"), P(("space", "tile"), None, None, None)),
        check_vma=False,
    )
```

```python
import functools
import math

import jax
import jax.numpy as jnp
from jax import lax
from jax.experimental import pallas as pl
from jax.experimental.pallas import tpu as pltpu
from jax.sharding import PartitionSpec as P

NEV = 256
NC = 3
SPIN = 4
NMOM = 2
EDGE = 64
NX, NY, NZ = 4, 4, 8
PLANE = NX * NY
RANKS = 2 * PLANE
NSPACE = NX * NZ
BLOCK = 128
KDEV = 16
MESH = pl.DeviceIdType.MESH
PLANE_FAR = tuple(
    sorted(
        ((dx, dy) for dx in range(NX) for dy in range(NY) if dx or dy),
        key=lambda d: -min(d[0], NX - d[0]) - min(d[1], NY - d[1]),
    )
)
F32 = jnp.float32
BF16 = jnp.bfloat16
NT = (((1,), (1,)), ((), ()))
TN = (((0,), (0,)), ((), ()))


def split(v):
    hi = v.astype(BF16)
    return hi, (v - hi.astype(F32)).astype(BF16)


def dot(a, b, dims=NT):
    return lax.dot_general(a, b, dims, preferred_element_type=F32)


def kernel(
    momenta_in, graphs_in, eig, sources_in, el_out, own_out, other_out,
    momenta, graphs, sources, el_ref, own_ref, vec, left, trig, acc, ebuf, stage, pair_in, plane_in, line_in, full, pick, picked, rows, rowed,
    tau_in, tau, tau_hi, tau_lo, wts, foreign,
    load_sem, own_sem, pair_send, pair_recv, plane_send, plane_recv, line_send, line_recv,
    pick_send, pick_recv, rows_send, rows_recv,
    ax_send, ax_recv, az_send, az_recv, bz_send, bz_recv, bx_send, bx_recv, push_send, push_recv, swap_send, swap_recv, small_sem, out_sem,
):
    space, tile = lax.axis_index("space"), lax.axis_index("tile")
    x, z = space // NZ, space % NZ
    y, core = tile // 2, tile % 2
    place = x * NY + y
    rank = core * PLANE + place
    me = space * (2 * NY) + tile
    sites = vec.shape[3]

    def at_plane(other_rank):
        c, q = other_rank // PLANE, other_rank % PLANE
        return ((q // NY) * NZ + z, (q % NY) * 2 + c)

    def at_z(zz):
        return (x * NZ + zz, tile)

    def at_x(xx):
        return (xx * NZ + z, tile)

    partner = (space, y * 2 + 1 - core)

    def mate_row(yy, c):
        return (yy + NY + 1 - 2 * ((yy + c) % 2)) % NY

    def remote(src, dst, send, recv, device):
        return pltpu.make_async_remote_copy(
            src_ref=src, dst_ref=dst, send_sem=send, recv_sem=recv, device_id=device, device_id_type=MESH
        )

    small = [
        pltpu.make_async_copy(momenta_in, momenta, small_sem.at[0]),
        pltpu.make_async_copy(sources_in, sources, small_sem.at[1]),
        pltpu.make_async_copy(graphs_in, graphs, small_sem.at[2]),
    ]
    for copy in small:
        copy.start()
    loads = [pltpu.make_async_copy(eig.at[:, c], vec.at[:, c], load_sem.at[c]) for c in range(NC)]
    for load in loads:
        load.start()

    barrier = pltpu.get_barrier_semaphore()

    for j in range(1, RANKS):
        pl.semaphore_signal(barrier, inc=1, device_id=at_plane((rank + j) % RANKS), device_id_type=MESH)
    for j in range(1, NZ):
        pl.semaphore_signal(barrier, inc=1, device_id=at_z((z + j) % NZ), device_id_type=MESH)

    a_a, a_b = 2 * core, 2 * core + 1
    slot = z * NX + x

    def phases():
        site = me * sites + 128 * lax.broadcasted_iota(jnp.int32, (8, 128), 0)
        site = site + lax.broadcasted_iota(jnp.int32, (8, 128), 1)
        px, py, pz = site & (EDGE - 1), (site >> 6) & (EDGE - 1), site >> 12
        for p in range(NMOM):
            wave = (momenta[p, 0] * px + momenta[p, 1] * py + momenta[p, 2] * pz) & (EDGE - 1)
            angle = wave.astype(F32) * (2.0 * math.pi / EDGE)
            for k, value in enumerate((jnp.cos(angle), jnp.sin(angle))):
                for row in range(8):
                    trig[p, k : k + 1, row * 128 : row * 128 + 128] = value[row : row + 1, :]

    def spread():
        half = SPIN * 128
        jj = lax.broadcasted_iota(jnp.int32, (half, half), 0)
        col = lax.broadcasted_iota(jnp.int32, (half, half), 1)
        ones = (((jj & 3) * 128 + (jj >> 2)) == col).astype(F32).astype(BF16)
        first = pl.multiple_of((y % 2) * KDEV, KDEV)
        for h in range(2):
            lanes = slice(h * half, (h + 1) * half)
            value = jnp.concatenate([sources[0, pl.ds(first, KDEV), lanes], sources[1, pl.ds(first, KDEV), lanes]], axis=0)
            hi = value.astype(BF16)
            rest = value - hi.astype(F32)
            mid = rest.astype(BF16)
            low = (rest - mid.astype(F32)).astype(BF16)
            nn = (((1,), (0,)), ((), ()))
            parts = dot(jnp.concatenate([hi, mid, low], axis=0), ones, nn)
            n = 2 * KDEV
            moved = parts[:n] + parts[n : 2 * n] + parts[2 * n :]
            for a in range(SPIN):
                for ri in range(2):
                    tau_in[a, ri, :, h * 128 : h * 128 + 128] = moved[
                        ri * KDEV : (ri + 1) * KDEV, a * 128 : a * 128 + 128
                    ]

    def go(copy):
        copy.start()

    def bundle(a, zz):
        return tau.at[a, pl.ds(zz * NX, NX)]

    def half_bundle(a, zz, h):
        return tau.at[a, pl.ds(zz * NX + h * (NX // 2), NX // 2)]

    def push(a, zz, k):
        go(remote(bundle(a, zz), bundle(a, zz), push_send.at[0], push_recv.at[0], partner))

    def waits(ref, sem):
        pltpu.make_async_copy(ref, ref, sem).wait()

    def b_along_x(zz, k):
        for j in range(1, NX):
            ref = tau.at[a_b, zz * NX + x]
            go(remote(ref, ref, bx_send.at[0], bx_recv.at[k], at_x((x + j) % NX)))

    def z_back(h):
        return (z + NZ - h) % NZ

    def z_on(h):
        return (z + h) % NZ

    def tau_first():
        own = [
            pltpu.make_async_copy(tau_in.at[a_a], tau.at[a_a, slot], own_sem.at[0]),
            pltpu.make_async_copy(tau_in.at[a_b], tau.at[a_b, slot], own_sem.at[1]),
        ]
        for copy in own:
            copy.start()
        for copy in own:
            copy.wait()
        for j in range(1, NX):
            ref = tau.at[a_a, slot]
            go(remote(ref, ref, ax_send.at[0], ax_recv.at[0], at_x((x + j) % NX)))
        ref = tau.at[a_b, slot]
        go(remote(ref, ref, bz_send.at[0], bz_recv.at[0, 0], at_z(z_on(1))))
        go(remote(ref, ref, bz_send.at[0], bz_recv.at[1, 0], at_z(z_back(1))))

    def b_z(h):
        up, down = z_back(h), z_on(h)
        ref_up, ref_down = tau.at[a_b, up * NX + x], tau.at[a_b, down * NX + x]
        if h < NZ // 2:
            waits(ref_up, bz_recv.at[0, h - 1])
            waits(ref_down, bz_recv.at[1, h - 1])
            if h + 1 == NZ // 2:
                ref_u, ref_d = ref_up.at[0], ref_down.at[1]
            else:
                ref_u, ref_d = ref_up, ref_down
            go(remote(ref_u, ref_u, bz_send.at[0], bz_recv.at[0, h], at_z(z_on(1))))
            go(remote(ref_d, ref_d, bz_send.at[0], bz_recv.at[1, h], at_z(z_back(1))))
            b_along_x(up, h)
            b_along_x(down, NZ // 2 + h)
        else:
            waits(ref_up.at[0], bz_recv.at[0, h - 1])
            waits(ref_up.at[1], bz_recv.at[1, h - 1])
            b_along_x(up, h)

    def b_push(k):
        zz = z_back(k) if k <= NZ // 2 else z_on(k - NZ // 2)
        waits(tau.at[a_b, pl.ds(0, NX - 1)], bx_recv.at[k])
        push(a_b, zz, NZ + k)

    def a_z(h, part):
        up, down = z_back(h), z_on(h)

        def onward(ref, way):
            to = at_z(z_on(1)) if way == 0 else at_z(z_back(1))
            go(remote(ref, ref, az_send.at[0], az_recv.at[way, h, part], to))

        def push_half(zz, k):
            ref = half_bundle(a_a, zz, part)
            go(remote(ref, ref, push_send.at[0], push_recv.at[0], partner))

        if h == 0:
            if part == 0:
                waits(tau.at[a_a, pl.ds(0, NX - 1)], ax_recv.at[0])
            onward(half_bundle(a_a, z, part), 0)
            onward(half_bundle(a_a, z, part), 1)
            push_half(z, 0)
        elif h < NZ // 2:
            waits(half_bundle(a_a, up, part), az_recv.at[0, h - 1, part])
            waits(half_bundle(a_a, down, part), az_recv.at[1, h - 1, part])
            if h + 1 < NZ // 2 or part == 0:
                onward(half_bundle(a_a, up, part), 0)
            if h + 1 < NZ // 2 or part == 1:
                onward(half_bundle(a_a, down, part), 1)
            push_half(up, h)
            push_half(down, NZ // 2 + h)
        else:
            waits(half_bundle(a_a, up, part), az_recv.at[part, h - 1, part])
            push_half(up, h)

    zero = space // NSPACE

    def gram(p, c):
        def body(c, _):
            r, i = vec[0, c], vec[1, c]
            co, si = trig[p, 0:1, :], trig[p, 1:2, :]
            wr = co * r + si * i
            wi = co * i - si * r
            for k, (lhs, rhs) in enumerate(((r, wr), (i, wi), (None, wr + wi))):
                if p == 0:
                    lh, ll = split(r - i if lhs is None else lhs)
                    left[k, c, :NEV] = lh
                    left[k, c, NEV:] = ll
                else:
                    lh, ll = left[k, c, :NEV], left[k, c, NEV:]
                rh, rl = split(rhs)
                wide = dot(jnp.concatenate([lh, ll], axis=0), rh)
                acc[k] += wide[:NEV] + wide[NEV:] + dot(lh, rl)
            return 0

        lax.fori_loop(zero + c, zero + c + 1, body, 0)

    def pair_copy(p):
        return remote(stage.at[p, 1 - core], pair_in.at[p], pair_send.at[p], pair_recv.at[p], partner)

    def finish_gram(p):
        p1, p2, p3 = acc[0], acc[1], acc[2]
        for ri, part in enumerate((p1 + p2, p3 - p1 + p2)):
            ebuf[ri, 0] = part[:, :128]
            ebuf[ri, 1] = part[:, 128:]
        for r in range(RANKS):
            for ri in range(2):
                for h in range(2):
                    lanes = pl.ds(h * 128, 128)
                    stage[p, r // PLANE, r % PLANE, ri, :, lanes] = ebuf[ri, h, pl.ds(r, 8, stride=32), :]
        go(pair_copy(p))

    def plane_stage(p):
        pair_copy(p).wait_recv()
        stage[p, core] += pair_in[p]

        for dx, dy in PLANE_FAR:
            q = ((x + dx) % NX) * NY + (y + dy) % NY
            remote(
                stage.at[p, core, q], plane_in.at[p, place], plane_send.at[p], plane_recv.at[p],
                at_plane(core * PLANE + q),
            ).start()
        plane_in[p, place] = stage[p, core, place]

    def line_stage(p):
        waits(plane_in.at[p, pl.ds(0, PLANE - 1)], plane_recv.at[p])
        total = plane_in[p, 0]
        for q in range(1, PLANE):
            total = total + plane_in[p, q]
        line_in[p, z] = total

        for dz in (4, 3, 5, 2, 6, 1, 7):
            ref = line_in.at[p, z]
            remote(ref, ref, line_send.at[p], line_recv.at[p], at_z((z + dz) % NZ)).start()

    def full_stage(p):
        waits(line_in.at[p, pl.ds(0, NZ - 1)], line_recv.at[p])
        total = line_in[p, 0]
        for q in range(1, NZ):
            total = total + line_in[p, q]
        for ri in range(2):
            full[p * 8 : p * 8 + 8, ri, :] = total[ri]

    def pick_stage(k):
        def fill(d):
            sp, tl = at_plane(d)
            yy, cc = tl // 2, tl % 2
            g = sp * (2 * NY) + (tl if k == 0 else mate_row(yy, cc) * 2 + cc)
            for m in range(2):
                value = full[graphs[m, g]]
                for h in range(2):
                    pick[k, d, h * 4 + m * 2 : h * 4 + m * 2 + 2, :] = value[:, h * 128 : h * 128 + 128]

        here = picked.at[k, pl.ds(pl.multiple_of(rank * 8, 8), 8)]
        for dx, dy in PLANE_FAR + ((0, 0),):
            for cc in (core, 1 - core):
                if (dx, dy) == (0, 0) and cc is core:
                    continue
                d = cc * PLANE + ((x + dx) % NX) * NY + (y + dy) % NY
                fill(d)
                remote(pick.at[k, d], here, pick_send.at[k], pick_recv.at[k], at_plane(d)).start()
        fill(rank)
        picked[k, pl.ds(pl.multiple_of(rank * 8, 8), 8), :] = pick[k, rank]

    def rows_stage():
        def send_rows(j, _):
            d = (rank + j) % RANKS
            _, tl = at_plane(d)
            rows[d, 0:2, :] = full[tl]
            rows[d, 2:4, :] = full[8 + tl]
            remote(rows.at[d], rowed.at[rank], rows_send.at[0], rows_recv.at[0], at_plane(d)).start()
            return 0

        lax.fori_loop(1, RANKS, send_rows, 0)
        rowed[rank, 0:2, :] = full[tile]
        rowed[rank, 2:4, :] = full[8 + tile]

    def convert(a):
        for s in range(NSPACE):
            for ri in range(2):
                hi, lo = split(tau[a, s, ri])
                tau_hi[a, ri, s * KDEV : (s + 1) * KDEV, :] = hi
                tau_lo[a, ri, s * KDEV : (s + 1) * KDEV, :] = lo

    norm = 1.0 / (NC * sites * NSPACE * 2 * NY)

    def moves(first_group):
        row = lax.broadcasted_iota(jnp.int32, (2 * BLOCK, 2 * BLOCK), 0)
        col = lax.broadcasted_iota(jnp.int32, (2 * BLOCK, 2 * BLOCK), 1)
        ri, a, i = row >> 7, row & 3, (row >> 2) & 31
        want = ri * BLOCK + ((a + first_group + ri) & 3) * 32 + i
        return (col == want).astype(F32).astype(BF16)

    def final():
        def weigh(k):
            waits(picked.at[k, pl.ds(0, 8 * RANKS - 8)], pick_recv.at[k])
            u_re, u_im, v_re, v_im = (
                jnp.concatenate([picked[k, pl.ds(4 * h + m, RANKS, stride=8), :] for h in range(2)], axis=1)
                for m in range(4)
            )
            for ri, values in enumerate(((u_re, u_im, v_re, v_im), (-u_im, u_re, -v_im, v_re))):
                for j, value in enumerate(values):
                    for part, half in enumerate(split(value)):
                        wts[ri, part, k, j * 32 : j * 32 + 32, :] = half
                        if j < 3:
                            wts[ri, part, k, j * 32 + BLOCK : j * 32 + BLOCK + 32, :] = half

        lane = lax.broadcasted_iota(jnp.int32, (1, BLOCK), 1)
        place_of = lane >> 5
        row_moves, col_moves = moves(0), moves(2)
        scale = norm / (NEV * math.sqrt(SPIN * NEV))
        nn = (((1,), (0,)), ((), ()))
        for k in (1, 0):
            weigh(k)
            groups = [None] * 4
            for a in range(SPIN):
                first = (-a % 4) * 32
                total = None
                for ri in range(2):
                    w_hi = wts[ri, 0, k, first : first + BLOCK, :]
                    both = jnp.concatenate([w_hi, wts[ri, 1, k, first : first + BLOCK, :]], axis=0)
                    wide = dot(tau_hi[a, ri], both)
                    new = wide[:, :BLOCK] + wide[:, BLOCK:] + dot(tau_lo[a, ri], w_hi)
                    total = new if total is None else total + new
                for g in range(4):
                    if groups[g] is None:
                        groups[g] = total
                    else:
                        groups[g] = jnp.where(place_of == (a + g) % 4, total, groups[g])
            uh, ul = split(jnp.concatenate([groups[0], groups[1]], axis=1))
            vh, vl = split(jnp.concatenate([groups[2], groups[3]], axis=1))
            c4 = dot(uh, vh, TN) + dot(uh, vl, TN) + dot(ul, vh, TN)
            hi, lo = split(c4 * scale)
            hi, lo = split(dot(row_moves, hi, nn) + dot(row_moves, lo, nn))
            c4 = dot(hi, col_moves) + dot(lo, col_moves)
            target = foreign if k == 1 else own_ref
            target[0] = c4[:BLOCK, :BLOCK] - c4[BLOCK:, BLOCK:]
            target[1] = c4[:BLOCK, BLOCK:] + c4[BLOCK:, :BLOCK]
            if k == 1:
                go(swap)

    mate = (space, mate_row(y, core) * 2 + core)
    swap = remote(foreign, other_out, swap_send.at[0], swap_recv.at[0], mate)

    def elementals():
        waits(rowed.at[pl.ds(0, RANKS - 1)], rows_recv.at[0])
        width8 = NEV // NSPACE
        col = lax.broadcasted_iota(jnp.int32, (width8, NEV), 0)
        lane = lax.broadcasted_iota(jnp.int32, (width8, NEV), 1)
        ones = (lane == space * width8 + col).astype(F32)
        for k in range(4):
            el_ref[k // 2, k % 2] = lax.dot_general(
                ones, rowed[:, k, :], NT, precision=lax.Precision.HIGHEST, preferred_element_type=F32
            )

    acc[...] = jnp.zeros_like(acc)
    small[0].wait()
    phases()
    loads[0].wait()
    gram(0, 0)
    small[1].wait()
    spread()
    small[2].wait()
    pl.semaphore_wait(barrier, RANKS - 1 + NZ - 1)
    tau_first()
    loads[1].wait()
    gram(0, 1)
    b_along_x(z, 0)
    loads[2].wait()
    gram(0, 2)
    finish_gram(0)
    acc[...] = jnp.zeros_like(acc)
    b_z(1)
    a_z(0, 0)
    a_z(0, 1)
    gram(1, 0)
    plane_stage(0)
    gram(1, 1)
    b_z(2)
    a_z(1, 0)
    b_push(0)
    gram(1, 2)
    finish_gram(1)
    a_z(1, 1)
    plane_stage(1)
    b_z(3)
    a_z(2, 0)
    b_push(1)
    b_push(5)
    line_stage(0)
    a_z(2, 1)
    b_z(4)
    a_z(3, 0)
    b_push(2)
    b_push(6)
    line_stage(1)
    a_z(3, 1)
    b_push(3)
    b_push(7)
    b_push(4)
    full_stage(0)
    a_z(4, 0)
    full_stage(1)
    pick_stage(1)
    pick_stage(0)
    a_z(4, 1)
    rows_stage()
    waits(tau.at[pl.ds(0, 2)], push_recv.at[0])
    for a in range(SPIN):
        convert(a)
    final()
    own_copy = pltpu.make_async_copy(own_ref, own_out, out_sem.at[0])
    own_copy.start()
    elementals()
    el_copy = pltpu.make_async_copy(el_ref, el_out, out_sem.at[1])
    el_copy.start()
    swap.wait_recv()
    own_copy.wait()
    el_copy.wait()
    waits(tau.at[0, pl.ds(0, NX - 1)], ax_send.at[0])
    waits(tau.at[0, pl.ds(0, NX * (NZ - 1))], az_send.at[0])
    waits(tau.at[0, pl.ds(0, NZ - 1)], bz_send.at[0])
    waits(tau.at[0, pl.ds(0, NZ * (NX - 1))], bx_send.at[0])
    waits(tau.at[pl.ds(0, 2)], push_send.at[0])
    swap.wait_send()
    for p in range(NMOM):
        pair_copy(p).wait_send()
        waits(plane_in.at[p, pl.ds(0, PLANE - 1)], plane_send.at[p])
        waits(line_in.at[p, pl.ds(0, NZ - 1)], line_send.at[p])
    for k in range(2):
        waits(picked.at[k, pl.ds(0, 8 * RANKS - 8)], pick_send.at[k])
    waits(rowed.at[pl.ds(0, RANKS - 1)], rows_send.at[0])


def per_device(eigenvectors, perambulator, momenta, graph_blocks):
    sites = eigenvectors.shape[3]
    eig = eigenvectors.transpose(0, 2, 1, 3)
    dma = pltpu.SemaphoreType.DMA
    width8 = NEV // NSPACE
    el, own, other = pl.pallas_call(
        kernel,
        out_shape=(
            jax.ShapeDtypeStruct((NMOM, 2, width8, 32), F32),
            jax.ShapeDtypeStruct((2, BLOCK, BLOCK), F32),
            jax.ShapeDtypeStruct((2, BLOCK, BLOCK), F32),
        ),
        in_specs=[
            pl.BlockSpec(memory_space=pltpu.HBM),
            pl.BlockSpec(memory_space=pltpu.HBM),
            pl.BlockSpec(memory_space=pltpu.HBM),
            pl.BlockSpec(memory_space=pltpu.HBM),
        ],
        out_specs=(pl.BlockSpec(memory_space=pl.ANY),) * 3,
        scratch_shapes=[
            pltpu.SMEM((NMOM, 3), jnp.int32),
            pltpu.SMEM((2, NSPACE * 2 * NY), jnp.int32),
            pltpu.VMEM((2, 2 * KDEV, SPIN * NEV), F32),
            pltpu.VMEM((NMOM, 2, width8, 32), F32),
            pltpu.VMEM((2, BLOCK, BLOCK), F32),
            pltpu.VMEM((2, NC, NEV, sites), F32),
            pltpu.VMEM((3, NC, 2 * NEV, sites), BF16),
            pltpu.VMEM((NMOM, 2, sites), F32),
            pltpu.VMEM((3, NEV, NEV), F32),
            pltpu.VMEM((2, 2, NEV, 128), F32),
            pltpu.VMEM((NMOM, 2, PLANE, 2, 8, NEV), F32),
            pltpu.VMEM((NMOM, PLANE, 2, 8, NEV), F32),
            pltpu.VMEM((NMOM, PLANE, 2, 8, NEV), F32),
            pltpu.VMEM((NMOM, NZ, 2, 8, NEV), F32),
            pltpu.VMEM((16, 2, NEV), F32),
            pltpu.VMEM((2, RANKS, 8, 128), F32),
            pltpu.VMEM((2, RANKS * 8, 128), F32),
            pltpu.VMEM((RANKS, 4, NEV), F32),
            pltpu.VMEM((RANKS, 4, NEV), F32),
            pltpu.VMEM((SPIN, 2, KDEV, NEV), F32),
            pltpu.VMEM((SPIN, NSPACE, 2, KDEV, NEV), F32),
            pltpu.VMEM((SPIN, 2, NSPACE * KDEV, NEV), BF16),
            pltpu.VMEM((SPIN, 2, NSPACE * KDEV, NEV), BF16),
            pltpu.VMEM((2, 2, 2, 7 * 32, NEV), BF16),
            pltpu.VMEM((2, BLOCK, BLOCK), F32),
            dma((NC,)),
            dma((2,)),
            dma((NMOM,)),
            dma((NMOM,)),
            dma((NMOM,)),
            dma((NMOM,)),
            dma((NMOM,)),
            dma((NMOM,)),
            dma((2,)),
            dma((2,)),
            dma((1,)),
            dma((1,)),
            dma((1,)),
            dma((1,)),
            dma((1,)),
            dma((2, NZ // 2, 2)),
            dma((1,)),
            dma((2, NZ // 2)),
            dma((1,)),
            dma((NZ,)),
            dma((1,)),
            dma((1,)),
            dma((1,)),
            dma((1,)),
            dma((3,)),
            dma((2,)),
        ],
        compiler_params=pltpu.CompilerParams(
            collective_id=0, has_side_effects=True, vmem_limit_bytes=48 * 2**20
        ),
    )(*(pltpu.with_memory_space_constraint(v, pltpu.HBM) for v in (momenta, graph_blocks.T, eig, perambulator)))
    norm = 1.0 / math.sqrt(NC * sites * NSPACE * 2 * NY)

    def finish(el_ref, own_ref, other_ref, el_out, sum_out, el_buf, own_buf, other_buf, sems):
        pairs = ((own_ref, own_buf), (other_ref, other_buf), (el_ref, el_buf))
        copies = [pltpu.make_async_copy(a, b, sems.at[k]) for k, (a, b) in enumerate(pairs)]
        for copy in copies:
            copy.start()
        copies[0].wait()
        copies[1].wait()
        own_buf[...] += other_buf[...]
        sum_copy = pltpu.make_async_copy(own_buf, sum_out, sems.at[3])
        sum_copy.start()
        copies[2].wait()
        el_buf[...] *= norm
        el_copy = pltpu.make_async_copy(el_buf, el_out, sems.at[4])
        el_copy.start()
        sum_copy.wait()
        el_copy.wait()

    anywhere = pl.BlockSpec(memory_space=pl.ANY)
    hbm = pl.BlockSpec(memory_space=pltpu.HBM)
    el, out = pl.pallas_call(
        finish,
        out_shape=(jax.ShapeDtypeStruct(el.shape, F32), jax.ShapeDtypeStruct(own.shape, F32)),
        in_specs=[anywhere] * 3,
        out_specs=(hbm, hbm),
        scratch_shapes=[
            pltpu.VMEM(el.shape, F32),
            pltpu.VMEM(own.shape, F32),
            pltpu.VMEM(own.shape, F32),
            dma((5,)),
        ],
        compiler_params=pltpu.CompilerParams(vmem_limit_bytes=8 * 2**20),
    )(el, own, other)
    return el.transpose(0, 1, 3, 2), out[None]


def solution(mesh):
    return jax.shard_map(
        per_device,
        mesh=mesh,
        in_specs=(P(None, None, None, ("space", "tile")), P(None, "space", None), P(), P()),
        out_specs=(P(None, None, "tile", "space"), P(("space", "tile"), None, None, None)),
        check_vma=False,
    )
```

```python
import functools
import math

import jax
import jax.numpy as jnp
from jax import lax
from jax.experimental import pallas as pl
from jax.experimental.pallas import tpu as pltpu
from jax.sharding import PartitionSpec as P

NEV = 256
NC = 3
SPIN = 4
NMOM = 2
EDGE = 64
NX, NY, NZ = 4, 4, 8
PLANE = NX * NY
RANKS = 2 * PLANE
NSPACE = NX * NZ
BLOCK = 128
KDEV = 16
MESH = pl.DeviceIdType.MESH
PLANE_FAR = tuple(
    sorted(
        ((dx, dy) for dx in range(NX) for dy in range(NY) if dx or dy),
        key=lambda d: -min(d[0], NX - d[0]) - min(d[1], NY - d[1]),
    )
)
F32 = jnp.float32
BF16 = jnp.bfloat16
NT = (((1,), (1,)), ((), ()))
TN = (((0,), (0,)), ((), ()))


def split(v):
    hi = v.astype(BF16)
    return hi, (v - hi.astype(F32)).astype(BF16)


def dot(a, b, dims=NT):
    return lax.dot_general(a, b, dims, preferred_element_type=F32)


def kernel(
    momenta_in, graphs_in, eig, sources_in, el_out, own_out, other_out,
    momenta, graphs, sources, el_ref, own_ref, vec, left, trig, acc, ebuf, stage, pair_in, plane_in, line_in, full, pick, picked, rows, rowed,
    tau_in, tau, tau_hi, tau_lo, foreign,
    load_sem, own_sem, pair_send, pair_recv, plane_send, plane_recv, line_send, line_recv,
    pick_send, pick_recv, rows_send, rows_recv,
    ax_send, ax_recv, az_send, az_recv, bz_send, bz_recv, bx_send, bx_recv, push_send, push_recv, swap_send, swap_recv, small_sem, out_sem,
):
    space, tile = lax.axis_index("space"), lax.axis_index("tile")
    x, z = space // NZ, space % NZ
    y, core = tile // 2, tile % 2
    place = x * NY + y
    rank = core * PLANE + place
    me = space * (2 * NY) + tile
    sites = vec.shape[3]

    xs = [x] + [(x + d) % NX for d in range(1, NX)]
    ys = [y] + [(y + d) % NY for d in range(1, NY)]
    cores = (core, 1 - core)

    def plane_at(dx, dy, dc):
        return (xs[dx] * NZ + z, ys[dy] * 2 + cores[dc])

    def at_z(zz):
        return (x * NZ + zz, tile)

    def at_x(xx):
        return (xx * NZ + z, tile)

    partner = (space, y * 2 + 1 - core)

    def mate_row(yy, c):
        return (yy + NY + 1 - 2 * ((yy + c) % 2)) % NY

    mate_rows = [[mate_row(ys[dy], cores[dc]) for dc in range(2)] for dy in range(NY)]

    def remote(src, dst, send, recv, device):
        return pltpu.make_async_remote_copy(
            src_ref=src, dst_ref=dst, send_sem=send, recv_sem=recv, device_id=device, device_id_type=MESH
        )

    small = [
        pltpu.make_async_copy(momenta_in, momenta, small_sem.at[0]),
        pltpu.make_async_copy(
            sources_in.at[:, pl.ds(pl.multiple_of((y % 2) * KDEV, KDEV), KDEV)], sources, small_sem.at[1]
        ),
        pltpu.make_async_copy(graphs_in, graphs, small_sem.at[2]),
    ]
    for copy in small:
        copy.start()
    loads = [pltpu.make_async_copy(eig.at[:, c], vec.at[:, c], load_sem.at[c]) for c in range(NC)]
    loads[0].start()

    barrier = pltpu.get_barrier_semaphore()

    for dx, dy in PLANE_FAR + ((0, 0),):
        for dc in range(2):
            if dx or dy or dc:
                pl.semaphore_signal(barrier, inc=1, device_id=plane_at(dx, dy, dc), device_id_type=MESH)
    for j in range(1, NZ):
        pl.semaphore_signal(barrier, inc=1, device_id=at_z((z + j) % NZ), device_id_type=MESH)

    a_a, a_b = 2 * core, 2 * core + 1
    slot = z * NX + x

    def phases():
        site = me * sites + 128 * lax.broadcasted_iota(jnp.int32, (8, 128), 0)
        site = site + lax.broadcasted_iota(jnp.int32, (8, 128), 1)
        px, py, pz = site & (EDGE - 1), (site >> 6) & (EDGE - 1), site >> 12
        for p in range(NMOM):
            wave = (momenta[p, 0] * px + momenta[p, 1] * py + momenta[p, 2] * pz) & (EDGE - 1)
            angle = wave.astype(F32) * (2.0 * math.pi / EDGE)
            for k, value in enumerate((jnp.cos(angle), jnp.sin(angle))):
                for row in range(8):
                    trig[p, k : k + 1, row * 128 : row * 128 + 128] = value[row : row + 1, :]

    def spread():
        half = SPIN * 128
        jj = lax.broadcasted_iota(jnp.int32, (half, half), 0)
        col = lax.broadcasted_iota(jnp.int32, (half, half), 1)
        ones = (((jj & 3) * 128 + (jj >> 2)) == col).astype(F32).astype(BF16)
        for h in range(2):
            lanes = slice(h * half, (h + 1) * half)
            value = jnp.concatenate([sources[0, :, lanes], sources[1, :, lanes]], axis=0)
            hi = value.astype(BF16)
            rest = value - hi.astype(F32)
            mid = rest.astype(BF16)
            low = (rest - mid.astype(F32)).astype(BF16)
            nn = (((1,), (0,)), ((), ()))
            parts = dot(jnp.concatenate([hi, mid, low], axis=0), ones, nn)
            n = 2 * KDEV
            moved = parts[:n] + parts[n : 2 * n] + parts[2 * n :]
            for a in range(SPIN):
                for ri in range(2):
                    tau_in[a, ri, :, h * 128 : h * 128 + 128] = moved[
                        ri * KDEV : (ri + 1) * KDEV, a * 128 : a * 128 + 128
                    ]

    def go(copy):
        copy.start()

    def bundle(a, zz):
        return tau.at[a, pl.ds(zz * NX, NX)]

    def half_bundle(a, zz, h):
        return tau.at[a, pl.ds(zz * NX + h * (NX // 2), NX // 2)]

    def push(a, zz, k):
        go(remote(bundle(a, zz), bundle(a, zz), push_send.at[0], push_recv.at[0], partner))

    def waits(ref, sem):
        pltpu.make_async_copy(ref, ref, sem).wait()

    def b_along_x(zz, k):
        for j in range(1, NX):
            ref = tau.at[a_b, zz * NX + x]
            go(remote(ref, ref, bx_send.at[0], bx_recv.at[k], at_x((x + j) % NX)))

    def z_back(h):
        return (z + NZ - h) % NZ

    def z_on(h):
        return (z + h) % NZ

    def tau_first():
        own = [
            pltpu.make_async_copy(tau_in.at[a_a], tau.at[a_a, slot], own_sem.at[0]),
            pltpu.make_async_copy(tau_in.at[a_b], tau.at[a_b, slot], own_sem.at[1]),
        ]
        for copy in own:
            copy.start()
        for copy in own:
            copy.wait()
        for j in range(1, NX):
            ref = tau.at[a_a, slot]
            go(remote(ref, ref, ax_send.at[0], ax_recv.at[0], at_x((x + j) % NX)))
        ref = tau.at[a_b, slot]
        go(remote(ref, ref, bz_send.at[0], bz_recv.at[0, 0], at_z(z_on(1))))
        go(remote(ref, ref, bz_send.at[0], bz_recv.at[1, 0], at_z(z_back(1))))

    def b_z(h):
        up, down = z_back(h), z_on(h)
        ref_up, ref_down = tau.at[a_b, up * NX + x], tau.at[a_b, down * NX + x]
        if h < NZ // 2:
            waits(ref_up, bz_recv.at[0, h - 1])
            waits(ref_down, bz_recv.at[1, h - 1])
            if h + 1 == NZ // 2:
                ref_u, ref_d = ref_up.at[0], ref_down.at[1]
            else:
                ref_u, ref_d = ref_up, ref_down
            go(remote(ref_u, ref_u, bz_send.at[0], bz_recv.at[0, h], at_z(z_on(1))))
            go(remote(ref_d, ref_d, bz_send.at[0], bz_recv.at[1, h], at_z(z_back(1))))
        else:
            waits(ref_up.at[0], bz_recv.at[0, h - 1])
            waits(ref_up.at[1], bz_recv.at[1, h - 1])

    def b_x(h):
        b_along_x(z_back(h), h)
        if h < NZ // 2:
            b_along_x(z_on(h), NZ // 2 + h)

    def b_push(k):
        zz = z_back(k) if k <= NZ // 2 else z_on(k - NZ // 2)
        waits(tau.at[a_b, pl.ds(0, NX - 1)], bx_recv.at[k])
        push(a_b, zz, NZ + k)

    def a_z(h, part):
        up, down = z_back(h), z_on(h)

        def onward(ref, way):
            to = at_z(z_on(1)) if way == 0 else at_z(z_back(1))
            go(remote(ref, ref, az_send.at[0], az_recv.at[way, h, part], to))

        def push_half(zz, k):
            ref = half_bundle(a_a, zz, part)
            go(remote(ref, ref, push_send.at[0], push_recv.at[0], partner))

        if h == 0:
            if part == 0:
                waits(tau.at[a_a, pl.ds(0, NX - 1)], ax_recv.at[0])
            onward(half_bundle(a_a, z, part), 0)
            onward(half_bundle(a_a, z, part), 1)
            push_half(z, 0)
        elif h < NZ // 2:
            waits(half_bundle(a_a, up, part), az_recv.at[0, h - 1, part])
            waits(half_bundle(a_a, down, part), az_recv.at[1, h - 1, part])
            if h + 1 < NZ // 2 or part == 0:
                onward(half_bundle(a_a, up, part), 0)
            if h + 1 < NZ // 2 or part == 1:
                onward(half_bundle(a_a, down, part), 1)
            push_half(up, h)
            push_half(down, NZ // 2 + h)
        else:
            waits(half_bundle(a_a, up, part), az_recv.at[part, h - 1, part])
            push_half(up, h)

    zero = space // NSPACE

    def gram(p, c):
        def body(c, _):
            r, i = vec[0, c], vec[1, c]
            co, si = trig[p, 0:1, :], trig[p, 1:2, :]
            wr = co * r + si * i
            wi = co * i - si * r
            for k, (lhs, rhs) in enumerate(((r, wr), (i, wi), (None, wr + wi))):
                if p == 0:
                    lh, ll = split(r - i if lhs is None else lhs)
                    left[k, c, :NEV] = lh
                    left[k, c, NEV:] = ll
                else:
                    lh, ll = left[k, c, :NEV], left[k, c, NEV:]
                rh, rl = split(rhs)
                wide = dot(jnp.concatenate([lh, ll], axis=0), rh)
                acc[k] += wide[:NEV] + wide[NEV:] + dot(lh, rl)
            return 0

        lax.fori_loop(zero + c, zero + c + 1, body, 0)

    def pair_copy(p):
        return remote(stage.at[p, 1 - core], pair_in.at[p], pair_send.at[p], pair_recv.at[p], partner)

    def finish_gram(p):
        p1, p2, p3 = acc[0], acc[1], acc[2]
        for ri, part in enumerate((p1 + p2, p3 - p1 + p2)):
            ebuf[ri, 0] = part[:, :128]
            ebuf[ri, 1] = part[:, 128:]
        for r in range(RANKS):
            for ri in range(2):
                for h in range(2):
                    lanes = pl.ds(h * 128, 128)
                    stage[p, r // PLANE, r % PLANE, ri, :, lanes] = ebuf[ri, h, pl.ds(r, 8, stride=32), :]
        go(pair_copy(p))

    def plane_stage(p):
        pair_copy(p).wait_recv()
        stage[p, core] += pair_in[p]

        for dx, dy in PLANE_FAR:
            q = xs[dx] * NY + ys[dy]
            remote(
                stage.at[p, core, q], plane_in.at[p, place], plane_send.at[p], plane_recv.at[p],
                plane_at(dx, dy, 0),
            ).start()
        plane_in[p, place] = stage[p, core, place]

    def line_stage(p):
        waits(plane_in.at[p, pl.ds(0, PLANE - 1)], plane_recv.at[p])
        total = plane_in[p, 0]
        for q in range(1, PLANE):
            total = total + plane_in[p, q]
        line_in[p, z] = total

        for dz in (4, 3, 5, 2, 6, 1, 7):
            ref = line_in.at[p, z]
            remote(ref, ref, line_send.at[p], line_recv.at[p], at_z((z + dz) % NZ)).start()

    def full_stage(p):
        waits(line_in.at[p, pl.ds(0, NZ - 1)], line_recv.at[p])
        total = line_in[p, 0]
        for q in range(1, NZ):
            total = total + line_in[p, q]
        for ri in range(2):
            full[p * 8 : p * 8 + 8, ri, :] = total[ri]

    def pick_stage(k):
        def fill(dx, dy, dc):
            other_core = cores[dc]
            row = ys[dy] if k == 0 else mate_rows[dy][dc]
            g = (xs[dx] * NZ + z) * (2 * NY) + row * 2 + other_core
            d = other_core * PLANE + xs[dx] * NY + ys[dy]
            for m in range(2):
                value = full[graphs[m, g]]
                for h in range(2):
                    pick[k, d, h * 4 + m * 2 : h * 4 + m * 2 + 2, :] = value[:, h * 128 : h * 128 + 128]
            return d

        here = picked.at[k, pl.ds(pl.multiple_of(rank * 8, 8), 8)]
        for dx, dy in PLANE_FAR + ((0, 0),):
            for dc in range(2):
                if dx or dy or dc:
                    d = fill(dx, dy, dc)
                    remote(
                        pick.at[k, d], here, pick_send.at[k], pick_recv.at[k], plane_at(dx, dy, dc)
                    ).start()
        fill(0, 0, 0)
        picked[k, pl.ds(pl.multiple_of(rank * 8, 8), 8), :] = pick[k, rank]

    def rows_stage():
        for dx, dy in PLANE_FAR + ((0, 0),):
            for dc in range(2):
                if dx or dy or dc:
                    tl = ys[dy] * 2 + cores[dc]
                    d = cores[dc] * PLANE + xs[dx] * NY + ys[dy]
                    rows[d, 0:2, :] = full[tl]
                    rows[d, 2:4, :] = full[8 + tl]
                    remote(
                        rows.at[d], rowed.at[rank], rows_send.at[0], rows_recv.at[0], plane_at(dx, dy, dc)
                    ).start()
        rowed[rank, 0:2, :] = full[tile]
        rowed[rank, 2:4, :] = full[8 + tile]

    def convert(a):
        for s in range(NSPACE):
            for ri in range(2):
                hi, lo = split(tau[a, s, ri])
                tau_hi[a, ri, s * KDEV : (s + 1) * KDEV, :] = hi
                tau_lo[a, ri, s * KDEV : (s + 1) * KDEV, :] = lo

    norm = 1.0 / (NC * sites * NSPACE * 2 * NY)

    def final():
        row = lax.broadcasted_iota(jnp.int32, (BLOCK, BLOCK), 0)
        col = lax.broadcasted_iota(jnp.int32, (BLOCK, BLOCK), 1)
        moves = (col == (row & 3) * 32 + (row >> 2)).astype(F32).astype(BF16)
        scale = norm / (NEV * math.sqrt(SPIN * NEV))
        nn = (((1,), (0,)), ((), ()))
        for k in (1, 0):
            waits(picked.at[k, pl.ds(0, 8 * RANKS - 8)], pick_recv.at[k])
            u_re, u_im, v_re, v_im = (
                jnp.concatenate([picked[k, pl.ds(4 * h + m, RANKS, stride=8), :] for h in range(2)], axis=1)
                for m in range(4)
            )
            weights = []
            for values in ((u_re, u_im, v_re, v_im), (-u_im, u_re, -v_im, v_re)):
                hi, lo = split(jnp.concatenate(values, axis=0))
                weights.append((hi, jnp.concatenate([hi, lo], axis=0)))
            totals = []
            for a in range(SPIN):
                total = None
                for ri in range(2):
                    hi, both = weights[ri]
                    wide = dot(both, tau_hi[a, ri])
                    new = wide[:BLOCK] + wide[BLOCK:] + dot(hi, tau_lo[a, ri])
                    total = new if total is None else total + new
                totals.append(total)
            parts = [jnp.concatenate([t[g * 32 : g * 32 + 32] for t in totals], axis=0) for g in range(4)]
            uh, ul = split(jnp.concatenate(parts[:2], axis=0))
            vh, vl = split(jnp.concatenate(parts[2:], axis=0))
            c4 = dot(uh, vh) + dot(uh, vl) + dot(ul, vh)
            re = c4[:BLOCK, :BLOCK] - c4[BLOCK:, BLOCK:]
            im = c4[:BLOCK, BLOCK:] + c4[BLOCK:, :BLOCK]
            hi, lo = split(jnp.concatenate([re, im], axis=1) * scale)
            turned = dot(moves, hi, nn) + dot(moves, lo, nn)
            hi, lo = split(jnp.concatenate([turned[:, :BLOCK], turned[:, BLOCK:]], axis=0))
            result = dot(hi, moves) + dot(lo, moves)
            target = foreign if k == 1 else own_ref
            target[0] = result[:BLOCK]
            target[1] = result[BLOCK:]
            if k == 1:
                go(swap)

    mate = (space, mate_rows[0][0] * 2 + core)
    swap = remote(foreign, other_out, swap_send.at[0], swap_recv.at[0], mate)

    def elementals():
        waits(rowed.at[pl.ds(0, RANKS - 1)], rows_recv.at[0])
        width8 = NEV // NSPACE
        col = lax.broadcasted_iota(jnp.int32, (width8, NEV), 0)
        lane = lax.broadcasted_iota(jnp.int32, (width8, NEV), 1)
        ones = (lane == space * width8 + col).astype(F32)
        for k in range(4):
            el_ref[k // 2, k % 2] = lax.dot_general(
                ones, rowed[:, k, :], NT, precision=lax.Precision.HIGHEST, preferred_element_type=F32
            )

    loads[1].start()
    acc[...] = jnp.zeros_like(acc)
    small[0].wait()
    phases()
    small[1].wait()
    spread()
    loads[0].wait()
    loads[2].start()
    gram(0, 0)
    small[2].wait()
    pl.semaphore_wait(barrier, RANKS - 1 + NZ - 1)
    tau_first()
    loads[1].wait()
    gram(0, 1)
    b_along_x(z, 0)
    loads[2].wait()
    gram(0, 2)
    finish_gram(0)
    acc[...] = jnp.zeros_like(acc)
    gram(1, 0)
    plane_stage(0)
    b_z(1)
    a_z(0, 0)
    a_z(0, 1)
    b_x(1)
    gram(1, 1)
    gram(1, 2)
    finish_gram(1)
    plane_stage(1)
    b_z(2)
    a_z(1, 0)
    a_z(1, 1)
    b_x(2)
    b_push(0)
    line_stage(0)
    a_z(2, 0)
    b_z(3)
    b_x(3)
    b_push(1)
    b_push(5)
    line_stage(1)
    a_z(2, 1)
    b_z(4)
    b_x(4)
    a_z(3, 0)
    b_push(2)
    b_push(6)
    a_z(3, 1)
    full_stage(0)
    full_stage(1)
    pick_stage(1)
    pick_stage(0)
    a_z(4, 0)
    a_z(4, 1)
    b_push(3)
    b_push(7)
    b_push(4)
    rows_stage()
    waits(tau.at[pl.ds(0, 2)], push_recv.at[0])
    for a in range(SPIN):
        convert(a)
    final()
    own_copy = pltpu.make_async_copy(own_ref, own_out, out_sem.at[0])
    own_copy.start()
    elementals()
    el_copy = pltpu.make_async_copy(el_ref, el_out, out_sem.at[1])
    el_copy.start()
    swap.wait_recv()
    own_copy.wait()
    el_copy.wait()
    waits(tau.at[0, pl.ds(0, NX - 1)], ax_send.at[0])
    waits(tau.at[0, pl.ds(0, NX * (NZ - 1))], az_send.at[0])
    waits(tau.at[0, pl.ds(0, NZ - 1)], bz_send.at[0])
    waits(tau.at[0, pl.ds(0, NZ * (NX - 1))], bx_send.at[0])
    waits(tau.at[pl.ds(0, 2)], push_send.at[0])
    swap.wait_send()
    for p in range(NMOM):
        pair_copy(p).wait_send()
        waits(plane_in.at[p, pl.ds(0, PLANE - 1)], plane_send.at[p])
        waits(line_in.at[p, pl.ds(0, NZ - 1)], line_send.at[p])
    for k in range(2):
        waits(picked.at[k, pl.ds(0, 8 * RANKS - 8)], pick_send.at[k])
    waits(rowed.at[pl.ds(0, RANKS - 1)], rows_send.at[0])


def per_device(eigenvectors, perambulator, momenta, graph_blocks):
    sites = eigenvectors.shape[3]
    eig = eigenvectors.transpose(0, 2, 1, 3)
    dma = pltpu.SemaphoreType.DMA
    width8 = NEV // NSPACE
    el, own, other = pl.pallas_call(
        kernel,
        out_shape=(
            jax.ShapeDtypeStruct((NMOM, 2, width8, 32), F32),
            jax.ShapeDtypeStruct((2, BLOCK, BLOCK), F32),
            jax.ShapeDtypeStruct((2, BLOCK, BLOCK), F32),
        ),
        in_specs=[
            pl.BlockSpec(memory_space=pltpu.HBM),
            pl.BlockSpec(memory_space=pltpu.HBM),
            pl.BlockSpec(memory_space=pltpu.HBM),
            pl.BlockSpec(memory_space=pltpu.HBM),
        ],
        out_specs=(pl.BlockSpec(memory_space=pl.ANY),) * 3,
        scratch_shapes=[
            pltpu.SMEM((NMOM, 3), jnp.int32),
            pltpu.SMEM((2, NSPACE * 2 * NY), jnp.int32),
            pltpu.VMEM((2, KDEV, SPIN * NEV), F32),
            pltpu.VMEM((NMOM, 2, width8, 32), F32),
            pltpu.VMEM((2, BLOCK, BLOCK), F32),
            pltpu.VMEM((2, NC, NEV, sites), F32),
            pltpu.VMEM((3, NC, 2 * NEV, sites), BF16),
            pltpu.VMEM((NMOM, 2, sites), F32),
            pltpu.VMEM((3, NEV, NEV), F32),
            pltpu.VMEM((2, 2, NEV, 128), F32),
            pltpu.VMEM((NMOM, 2, PLANE, 2, 8, NEV), F32),
            pltpu.VMEM((NMOM, PLANE, 2, 8, NEV), F32),
            pltpu.VMEM((NMOM, PLANE, 2, 8, NEV), F32),
            pltpu.VMEM((NMOM, NZ, 2, 8, NEV), F32),
            pltpu.VMEM((16, 2, NEV), F32),
            pltpu.VMEM((2, RANKS, 8, 128), F32),
            pltpu.VMEM((2, RANKS * 8, 128), F32),
            pltpu.VMEM((RANKS, 4, NEV), F32),
            pltpu.VMEM((RANKS, 4, NEV), F32),
            pltpu.VMEM((SPIN, 2, KDEV, NEV), F32),
            pltpu.VMEM((SPIN, NSPACE, 2, KDEV, NEV), F32),
            pltpu.VMEM((SPIN, 2, NSPACE * KDEV, NEV), BF16),
            pltpu.VMEM((SPIN, 2, NSPACE * KDEV, NEV), BF16),
            pltpu.VMEM((2, BLOCK, BLOCK), F32),
            dma((NC,)),
            dma((2,)),
            dma((NMOM,)),
            dma((NMOM,)),
            dma((NMOM,)),
            dma((NMOM,)),
            dma((NMOM,)),
            dma((NMOM,)),
            dma((2,)),
            dma((2,)),
            dma((1,)),
            dma((1,)),
            dma((1,)),
            dma((1,)),
            dma((1,)),
            dma((2, NZ // 2, 2)),
            dma((1,)),
            dma((2, NZ // 2)),
            dma((1,)),
            dma((NZ,)),
            dma((1,)),
            dma((1,)),
            dma((1,)),
            dma((1,)),
            dma((3,)),
            dma((2,)),
        ],
        compiler_params=pltpu.CompilerParams(
            collective_id=0, has_side_effects=True, vmem_limit_bytes=48 * 2**20
        ),
    )(*(pltpu.with_memory_space_constraint(v, pltpu.HBM) for v in (momenta, graph_blocks.T, eig, perambulator)))
    norm = 1.0 / math.sqrt(NC * sites * NSPACE * 2 * NY)

    def finish(el_ref, own_ref, other_ref, el_out, sum_out, el_buf, own_buf, other_buf, sems):
        pairs = ((own_ref, own_buf), (other_ref, other_buf), (el_ref, el_buf))
        copies = [pltpu.make_async_copy(a, b, sems.at[k]) for k, (a, b) in enumerate(pairs)]
        for copy in copies:
            copy.start()
        copies[0].wait()
        copies[1].wait()
        own_buf[...] += other_buf[...]
        sum_copy = pltpu.make_async_copy(own_buf, sum_out, sems.at[3])
        sum_copy.start()
        copies[2].wait()
        el_buf[...] *= norm
        el_copy = pltpu.make_async_copy(el_buf, el_out, sems.at[4])
        el_copy.start()
        sum_copy.wait()
        el_copy.wait()

    anywhere = pl.BlockSpec(memory_space=pl.ANY)
    hbm = pl.BlockSpec(memory_space=pltpu.HBM)
    el, out = pl.pallas_call(
        finish,
        out_shape=(jax.ShapeDtypeStruct(el.shape, F32), jax.ShapeDtypeStruct(own.shape, F32)),
        in_specs=[anywhere] * 3,
        out_specs=(hbm, hbm),
        scratch_shapes=[
            pltpu.VMEM(el.shape, F32),
            pltpu.VMEM(own.shape, F32),
            pltpu.VMEM(own.shape, F32),
            dma((5,)),
        ],
        compiler_params=pltpu.CompilerParams(vmem_limit_bytes=8 * 2**20),
    )(el, own, other)
    return el.transpose(0, 1, 3, 2), out[None]


def solution(mesh):
    return jax.shard_map(
        per_device,
        mesh=mesh,
        in_specs=(P(None, None, None, ("space", "tile")), P(None, "space", None), P(), P()),
        out_specs=(P(None, None, "tile", "space"), P(("space", "tile"), None, None, None)),
        check_vma=False,
    )
```

```python
import functools
import math

import jax
import jax.numpy as jnp
from jax import lax
from jax.experimental import pallas as pl
from jax.experimental.pallas import tpu as pltpu
from jax.sharding import PartitionSpec as P

NEV = 256
NC = 3
SPIN = 4
NMOM = 2
EDGE = 64
NX, NY, NZ = 4, 4, 8
PLANE = NX * NY
RANKS = 2 * PLANE
NSPACE = NX * NZ
BLOCK = 128
KDEV = 16
MESH = pl.DeviceIdType.MESH
PLANE_FAR = tuple(
    sorted(
        ((dx, dy) for dx in range(NX) for dy in range(NY) if dx or dy),
        key=lambda d: -min(d[0], NX - d[0]) - min(d[1], NY - d[1]),
    )
)
F32 = jnp.float32
BF16 = jnp.bfloat16
NT = (((1,), (1,)), ((), ()))
TN = (((0,), (0,)), ((), ()))


def split(v):
    hi = v.astype(BF16)
    return hi, (v - hi.astype(F32)).astype(BF16)


def dot(a, b, dims=NT):
    return lax.dot_general(a, b, dims, preferred_element_type=F32)


def kernel(
    momenta_in, graphs_in, eig, sources_in, el_out, own_out, other_out,
    momenta, graphs, sources, el_ref, own_ref, vec, left, trig, acc, ebuf, stage, pair_in, plane_in, line_in, full, pick, picked, rows, rowed,
    tau_in, tau, tau_hi, tau_lo, foreign,
    load_sem, own_sem, pair_send, pair_recv, plane_send, plane_recv, line_send, line_recv,
    pick_send, pick_recv, rows_send, rows_recv,
    ax_send, ax_recv, az_send, az_recv, bz_send, bz_recv, bx_send, bx_recv, push_send, push_recv, swap_send, swap_recv, small_sem, out_sem,
):
    space, tile = lax.axis_index("space"), lax.axis_index("tile")
    x, z = space // NZ, space % NZ
    y, core = tile // 2, tile % 2
    place = x * NY + y
    rank = core * PLANE + place
    me = space * (2 * NY) + tile
    sites = vec.shape[3]

    xs = [x] + [(x + d) % NX for d in range(1, NX)]
    ys = [y] + [(y + d) % NY for d in range(1, NY)]
    cores = (core, 1 - core)

    def plane_at(dx, dy, dc):
        return (xs[dx] * NZ + z, ys[dy] * 2 + cores[dc])

    def at_z(zz):
        return (x * NZ + zz, tile)

    def at_x(xx):
        return (xx * NZ + z, tile)

    partner = (space, y * 2 + 1 - core)

    def mate_row(yy, c):
        return (yy + NY + 1 - 2 * ((yy + c) % 2)) % NY

    mate_rows = [[mate_row(ys[dy], cores[dc]) for dc in range(2)] for dy in range(NY)]

    def remote(src, dst, send, recv, device):
        return pltpu.make_async_remote_copy(
            src_ref=src, dst_ref=dst, send_sem=send, recv_sem=recv, device_id=device, device_id_type=MESH
        )

    small = [
        pltpu.make_async_copy(momenta_in, momenta, small_sem.at[0]),
        pltpu.make_async_copy(
            sources_in.at[:, pl.ds(pl.multiple_of((y % 2) * KDEV, KDEV), KDEV)], sources, small_sem.at[1]
        ),
        pltpu.make_async_copy(graphs_in, graphs, small_sem.at[2]),
    ]
    for copy in small:
        copy.start()
    loads = [pltpu.make_async_copy(eig.at[:, c], vec.at[:, c], load_sem.at[c]) for c in range(NC)]
    loads[0].start()

    barrier = pltpu.get_barrier_semaphore()

    for dx, dy in PLANE_FAR + ((0, 0),):
        for dc in range(2):
            if dx or dy or dc:
                pl.semaphore_signal(barrier, inc=1, device_id=plane_at(dx, dy, dc), device_id_type=MESH)
    for j in range(1, NZ):
        pl.semaphore_signal(barrier, inc=1, device_id=at_z((z + j) % NZ), device_id_type=MESH)

    a_a, a_b = 2 * core, 2 * core + 1
    slot = z * NX + x

    def phases():
        site = me * sites + 128 * lax.broadcasted_iota(jnp.int32, (8, 128), 0)
        site = site + lax.broadcasted_iota(jnp.int32, (8, 128), 1)
        px, py, pz = site & (EDGE - 1), (site >> 6) & (EDGE - 1), site >> 12
        for p in range(NMOM):
            wave = (momenta[p, 0] * px + momenta[p, 1] * py + momenta[p, 2] * pz) & (EDGE - 1)
            angle = wave.astype(F32) * (2.0 * math.pi / EDGE)
            for k, value in enumerate((jnp.cos(angle), jnp.sin(angle))):
                for row in range(8):
                    trig[p, k : k + 1, row * 128 : row * 128 + 128] = value[row : row + 1, :]

    def spread():
        half = SPIN * 128
        jj = lax.broadcasted_iota(jnp.int32, (half, half), 0)
        col = lax.broadcasted_iota(jnp.int32, (half, half), 1)
        ones = (((jj & 3) * 128 + (jj >> 2)) == col).astype(F32).astype(BF16)
        for h in range(2):
            lanes = slice(h * half, (h + 1) * half)
            value = jnp.concatenate([sources[0, :, lanes], sources[1, :, lanes]], axis=0)
            hi = value.astype(BF16)
            rest = value - hi.astype(F32)
            mid = rest.astype(BF16)
            low = (rest - mid.astype(F32)).astype(BF16)
            nn = (((1,), (0,)), ((), ()))
            parts = dot(jnp.concatenate([hi, mid, low], axis=0), ones, nn)
            n = 2 * KDEV
            moved = parts[:n] + parts[n : 2 * n] + parts[2 * n :]
            for a in range(SPIN):
                for ri in range(2):
                    tau_in[a, ri, :, h * 128 : h * 128 + 128] = moved[
                        ri * KDEV : (ri + 1) * KDEV, a * 128 : a * 128 + 128
                    ]

    def go(copy):
        copy.start()

    def bundle(a, zz):
        return tau.at[a, pl.ds(zz * NX, NX)]

    def half_bundle(a, zz, h):
        return tau.at[a, pl.ds(zz * NX + h * (NX // 2), NX // 2)]

    def push(a, zz, k):
        go(remote(bundle(a, zz), bundle(a, zz), push_send.at[0], push_recv.at[0], partner))

    def waits(ref, sem):
        pltpu.make_async_copy(ref, ref, sem).wait()

    def b_along_x(zz, k):
        for j in range(1, NX):
            ref = tau.at[a_b, zz * NX + x]
            go(remote(ref, ref, bx_send.at[0], bx_recv.at[k], at_x((x + j) % NX)))

    def z_back(h):
        return (z + NZ - h) % NZ

    def z_on(h):
        return (z + h) % NZ

    def tau_first():
        own = [
            pltpu.make_async_copy(tau_in.at[a_a], tau.at[a_a, slot], own_sem.at[0]),
            pltpu.make_async_copy(tau_in.at[a_b], tau.at[a_b, slot], own_sem.at[1]),
        ]
        for copy in own:
            copy.start()
        for copy in own:
            copy.wait()
        for j in range(1, NX):
            ref = tau.at[a_a, slot]
            go(remote(ref, ref, ax_send.at[0], ax_recv.at[0], at_x((x + j) % NX)))
        ref = tau.at[a_b, slot]
        go(remote(ref, ref, bz_send.at[0], bz_recv.at[0, 0], at_z(z_on(1))))
        go(remote(ref, ref, bz_send.at[0], bz_recv.at[1, 0], at_z(z_back(1))))

    def b_z(h):
        up, down = z_back(h), z_on(h)
        ref_up, ref_down = tau.at[a_b, up * NX + x], tau.at[a_b, down * NX + x]
        if h < NZ // 2:
            waits(ref_up, bz_recv.at[0, h - 1])
            waits(ref_down, bz_recv.at[1, h - 1])
            if h + 1 == NZ // 2:
                ref_u, ref_d = ref_up.at[0], ref_down.at[1]
            else:
                ref_u, ref_d = ref_up, ref_down
            go(remote(ref_u, ref_u, bz_send.at[0], bz_recv.at[0, h], at_z(z_on(1))))
            go(remote(ref_d, ref_d, bz_send.at[0], bz_recv.at[1, h], at_z(z_back(1))))
        else:
            waits(ref_up.at[0], bz_recv.at[0, h - 1])
            waits(ref_up.at[1], bz_recv.at[1, h - 1])

    def b_x(h):
        b_along_x(z_back(h), h)
        if h < NZ // 2:
            b_along_x(z_on(h), NZ // 2 + h)

    def b_push(k):
        zz = z_back(k) if k <= NZ // 2 else z_on(k - NZ // 2)
        waits(tau.at[a_b, pl.ds(0, NX - 1)], bx_recv.at[k])
        push(a_b, zz, NZ + k)

    def a_z(h, part):
        up, down = z_back(h), z_on(h)

        def onward(ref, way):
            to = at_z(z_on(1)) if way == 0 else at_z(z_back(1))
            go(remote(ref, ref, az_send.at[0], az_recv.at[way, h, part], to))

        def push_half(zz, k):
            ref = half_bundle(a_a, zz, part)
            go(remote(ref, ref, push_send.at[0], push_recv.at[0], partner))

        if h == 0:
            if part == 0:
                waits(tau.at[a_a, pl.ds(0, NX - 1)], ax_recv.at[0])
            onward(half_bundle(a_a, z, part), 0)
            onward(half_bundle(a_a, z, part), 1)
            push_half(z, 0)
        elif h < NZ // 2:
            waits(half_bundle(a_a, up, part), az_recv.at[0, h - 1, part])
            waits(half_bundle(a_a, down, part), az_recv.at[1, h - 1, part])
            if h + 1 < NZ // 2 or part == 0:
                onward(half_bundle(a_a, up, part), 0)
            if h + 1 < NZ // 2 or part == 1:
                onward(half_bundle(a_a, down, part), 1)
            push_half(up, h)
            push_half(down, NZ // 2 + h)
        else:
            waits(half_bundle(a_a, up, part), az_recv.at[part, h - 1, part])
            push_half(up, h)

    zero = space // NSPACE

    def gram(p, c):
        def body(c, _):
            r, i = vec[0, c], vec[1, c]
            co, si = trig[p, 0:1, :], trig[p, 1:2, :]
            wr = co * r + si * i
            wi = co * i - si * r
            for k, (lhs, rhs) in enumerate(((r, wr), (i, wi), (None, wr + wi))):
                if p == 0:
                    lh, ll = split(r - i if lhs is None else lhs)
                    left[k, c, :NEV] = lh
                    left[k, c, NEV:] = ll
                else:
                    lh, ll = left[k, c, :NEV], left[k, c, NEV:]
                rh, rl = split(rhs)
                wide = dot(jnp.concatenate([lh, ll], axis=0), rh)
                acc[k] += wide[:NEV] + wide[NEV:] + dot(lh, rl)
            return 0

        lax.fori_loop(zero + c, zero + c + 1, body, 0)

    def pair_copy(p):
        return remote(stage.at[p, 1 - core], pair_in.at[p], pair_send.at[p], pair_recv.at[p], partner)

    def finish_gram(p):
        p1, p2, p3 = acc[0], acc[1], acc[2]
        for ri, part in enumerate((p1 + p2, p3 - p1 + p2)):
            ebuf[ri, 0] = part[:, :128]
            ebuf[ri, 1] = part[:, 128:]
        for r in range(RANKS):
            for ri in range(2):
                for h in range(2):
                    lanes = pl.ds(h * 128, 128)
                    stage[p, r // PLANE, r % PLANE, ri, :, lanes] = ebuf[ri, h, pl.ds(r, 8, stride=32), :]
        go(pair_copy(p))

    def plane_stage(p):
        pair_copy(p).wait_recv()
        stage[p, core] += pair_in[p]

        for dx, dy in PLANE_FAR:
            q = xs[dx] * NY + ys[dy]
            remote(
                stage.at[p, core, q], plane_in.at[p, place], plane_send.at[p], plane_recv.at[p],
                plane_at(dx, dy, 0),
            ).start()
        plane_in[p, place] = stage[p, core, place]

    def line_stage(p):
        waits(plane_in.at[p, pl.ds(0, PLANE - 1)], plane_recv.at[p])
        total = plane_in[p, 0]
        for q in range(1, PLANE):
            total = total + plane_in[p, q]
        line_in[p, z] = total

        for dz in (4, 3, 5, 2, 6, 1, 7):
            ref = line_in.at[p, z]
            remote(ref, ref, line_send.at[p], line_recv.at[p], at_z((z + dz) % NZ)).start()

    def full_stage(p):
        waits(line_in.at[p, pl.ds(0, NZ - 1)], line_recv.at[p])
        total = line_in[p, 0]
        for q in range(1, NZ):
            total = total + line_in[p, q]
        for ri in range(2):
            full[p * 8 : p * 8 + 8, ri, :] = total[ri]

    def pick_stage(k):
        def fill(dx, dy, dc):
            other_core = cores[dc]
            row = ys[dy] if k == 0 else mate_rows[dy][dc]
            g = (xs[dx] * NZ + z) * (2 * NY) + row * 2 + other_core
            d = other_core * PLANE + xs[dx] * NY + ys[dy]
            for m in range(2):
                value = full[graphs[m, g]]
                for h in range(2):
                    pick[k, d, h * 4 + m * 2 : h * 4 + m * 2 + 2, :] = value[:, h * 128 : h * 128 + 128]
            return d

        here = picked.at[k, pl.ds(pl.multiple_of(rank * 8, 8), 8)]
        for dx, dy in PLANE_FAR + ((0, 0),):
            for dc in range(2):
                if dx or dy or dc:
                    d = fill(dx, dy, dc)
                    remote(
                        pick.at[k, d], here, pick_send.at[k], pick_recv.at[k], plane_at(dx, dy, dc)
                    ).start()
        fill(0, 0, 0)
        picked[k, pl.ds(pl.multiple_of(rank * 8, 8), 8), :] = pick[k, rank]

    def rows_stage():
        for dx, dy in PLANE_FAR + ((0, 0),):
            for dc in range(2):
                if dx or dy or dc:
                    tl = ys[dy] * 2 + cores[dc]
                    d = cores[dc] * PLANE + xs[dx] * NY + ys[dy]
                    rows[d, 0:2, :] = full[tl]
                    rows[d, 2:4, :] = full[8 + tl]
                    remote(
                        rows.at[d], rowed.at[rank], rows_send.at[0], rows_recv.at[0], plane_at(dx, dy, dc)
                    ).start()
        rowed[rank, 0:2, :] = full[tile]
        rowed[rank, 2:4, :] = full[8 + tile]

    def convert(a):
        for s in range(NSPACE):
            for ri in range(2):
                hi, lo = split(tau[a, s, ri])
                tau_hi[a, ri, s * KDEV : (s + 1) * KDEV, :] = hi
                tau_lo[a, ri, s * KDEV : (s + 1) * KDEV, :] = lo

    norm = 1.0 / (NC * sites * NSPACE * 2 * NY)

    def final():
        row = lax.broadcasted_iota(jnp.int32, (BLOCK, BLOCK), 0)
        col = lax.broadcasted_iota(jnp.int32, (BLOCK, BLOCK), 1)
        moves = (col == (row & 3) * 32 + (row >> 2)).astype(F32).astype(BF16)
        scale = norm / (NEV * math.sqrt(SPIN * NEV))
        nn = (((1,), (0,)), ((), ()))
        for k in (1, 0):
            waits(picked.at[k, pl.ds(0, 8 * RANKS - 8)], pick_recv.at[k])
            u_re, u_im, v_re, v_im = (
                jnp.concatenate([picked[k, pl.ds(4 * h + m, RANKS, stride=8), :] for h in range(2)], axis=1)
                for m in range(4)
            )
            weights = []
            for values in ((u_re, u_im, v_re, v_im), (-u_im, u_re, -v_im, v_re)):
                hi, lo = split(jnp.concatenate(values, axis=0))
                weights.append((hi, jnp.concatenate([hi, lo], axis=0)))
            totals = []
            for a in range(SPIN):
                total = None
                for ri in range(2):
                    hi, both = weights[ri]
                    wide = dot(both, tau_hi[a, ri])
                    new = wide[:BLOCK] + wide[BLOCK:] + dot(hi, tau_lo[a, ri])
                    total = new if total is None else total + new
                totals.append(total)
            parts = [jnp.concatenate([t[g * 32 : g * 32 + 32] for t in totals], axis=0) for g in range(4)]
            uh, ul = split(jnp.concatenate(parts[:2], axis=0))
            vh, vl = split(jnp.concatenate(parts[2:], axis=0))
            c4 = dot(uh, vh) + dot(uh, vl) + dot(ul, vh)
            re = c4[:BLOCK, :BLOCK] - c4[BLOCK:, BLOCK:]
            im = c4[:BLOCK, BLOCK:] + c4[BLOCK:, :BLOCK]
            hi, lo = split(jnp.concatenate([re, im], axis=1) * scale)
            turned = dot(moves, hi, nn) + dot(moves, lo, nn)
            hi, lo = split(jnp.concatenate([turned[:, :BLOCK], turned[:, BLOCK:]], axis=0))
            result = dot(hi, moves) + dot(lo, moves)
            target = foreign if k == 1 else own_ref
            target[0] = result[:BLOCK]
            target[1] = result[BLOCK:]
            if k == 1:
                go(swap)

    mate = (space, mate_rows[0][0] * 2 + core)
    swap = remote(foreign, other_out, swap_send.at[0], swap_recv.at[0], mate)

    def elementals():
        waits(rowed.at[pl.ds(0, RANKS - 1)], rows_recv.at[0])
        width8 = NEV // NSPACE
        col = lax.broadcasted_iota(jnp.int32, (width8, NEV), 0)
        lane = lax.broadcasted_iota(jnp.int32, (width8, NEV), 1)
        ones = (lane == space * width8 + col).astype(F32)
        for k in range(4):
            el_ref[k // 2, k % 2] = lax.dot_general(
                ones, rowed[:, k, :], NT, precision=lax.Precision.HIGHEST, preferred_element_type=F32
            )

    loads[1].start()
    acc[...] = jnp.zeros_like(acc)
    small[0].wait()
    phases()
    small[1].wait()
    spread()
    loads[0].wait()
    loads[2].start()
    gram(0, 0)
    small[2].wait()
    pl.semaphore_wait(barrier, RANKS - 1 + NZ - 1)
    tau_first()
    loads[1].wait()
    gram(0, 1)
    b_along_x(z, 0)
    loads[2].wait()
    gram(0, 2)
    finish_gram(0)
    acc[...] = jnp.zeros_like(acc)
    a_z(0, 0)
    a_z(0, 1)
    gram(1, 0)
    plane_stage(0)
    b_z(1)
    b_x(1)
    gram(1, 1)
    gram(1, 2)
    finish_gram(1)
    a_z(1, 0)
    plane_stage(1)
    a_z(1, 1)
    b_z(2)
    b_x(2)
    b_push(0)
    line_stage(0)
    a_z(2, 0)
    b_z(3)
    b_x(3)
    a_z(2, 1)
    line_stage(1)
    b_push(1)
    b_push(5)
    a_z(3, 0)
    b_z(4)
    b_x(4)
    b_push(2)
    b_push(6)
    a_z(3, 1)
    full_stage(0)
    full_stage(1)
    pick_stage(1)
    pick_stage(0)
    a_z(4, 0)
    a_z(4, 1)
    b_push(3)
    b_push(7)
    b_push(4)
    rows_stage()
    waits(tau.at[pl.ds(0, 2)], push_recv.at[0])
    for a in range(SPIN):
        convert(a)
    final()
    own_copy = pltpu.make_async_copy(own_ref, own_out, out_sem.at[0])
    own_copy.start()
    elementals()
    el_copy = pltpu.make_async_copy(el_ref, el_out, out_sem.at[1])
    el_copy.start()
    swap.wait_recv()
    own_copy.wait()
    el_copy.wait()
    waits(tau.at[0, pl.ds(0, NX - 1)], ax_send.at[0])
    waits(tau.at[0, pl.ds(0, NX * (NZ - 1))], az_send.at[0])
    waits(tau.at[0, pl.ds(0, NZ - 1)], bz_send.at[0])
    waits(tau.at[0, pl.ds(0, NZ * (NX - 1))], bx_send.at[0])
    waits(tau.at[pl.ds(0, 2)], push_send.at[0])
    swap.wait_send()
    for p in range(NMOM):
        pair_copy(p).wait_send()
        waits(plane_in.at[p, pl.ds(0, PLANE - 1)], plane_send.at[p])
        waits(line_in.at[p, pl.ds(0, NZ - 1)], line_send.at[p])
    for k in range(2):
        waits(picked.at[k, pl.ds(0, 8 * RANKS - 8)], pick_send.at[k])
    waits(rowed.at[pl.ds(0, RANKS - 1)], rows_send.at[0])


def per_device(eigenvectors, perambulator, momenta, graph_blocks):
    sites = eigenvectors.shape[3]
    eig = eigenvectors.transpose(0, 2, 1, 3)
    dma = pltpu.SemaphoreType.DMA
    width8 = NEV // NSPACE
    el, own, other = pl.pallas_call(
        kernel,
        out_shape=(
            jax.ShapeDtypeStruct((NMOM, 2, width8, 32), F32),
            jax.ShapeDtypeStruct((2, BLOCK, BLOCK), F32),
            jax.ShapeDtypeStruct((2, BLOCK, BLOCK), F32),
        ),
        in_specs=[
            pl.BlockSpec(memory_space=pltpu.HBM),
            pl.BlockSpec(memory_space=pltpu.HBM),
            pl.BlockSpec(memory_space=pltpu.HBM),
            pl.BlockSpec(memory_space=pltpu.HBM),
        ],
        out_specs=(pl.BlockSpec(memory_space=pl.ANY),) * 3,
        scratch_shapes=[
            pltpu.SMEM((NMOM, 3), jnp.int32),
            pltpu.SMEM((2, NSPACE * 2 * NY), jnp.int32),
            pltpu.VMEM((2, KDEV, SPIN * NEV), F32),
            pltpu.VMEM((NMOM, 2, width8, 32), F32),
            pltpu.VMEM((2, BLOCK, BLOCK), F32),
            pltpu.VMEM((2, NC, NEV, sites), F32),
            pltpu.VMEM((3, NC, 2 * NEV, sites), BF16),
            pltpu.VMEM((NMOM, 2, sites), F32),
            pltpu.VMEM((3, NEV, NEV), F32),
            pltpu.VMEM((2, 2, NEV, 128), F32),
            pltpu.VMEM((NMOM, 2, PLANE, 2, 8, NEV), F32),
            pltpu.VMEM((NMOM, PLANE, 2, 8, NEV), F32),
            pltpu.VMEM((NMOM, PLANE, 2, 8, NEV), F32),
            pltpu.VMEM((NMOM, NZ, 2, 8, NEV), F32),
            pltpu.VMEM((16, 2, NEV), F32),
            pltpu.VMEM((2, RANKS, 8, 128), F32),
            pltpu.VMEM((2, RANKS * 8, 128), F32),
            pltpu.VMEM((RANKS, 4, NEV), F32),
            pltpu.VMEM((RANKS, 4, NEV), F32),
            pltpu.VMEM((SPIN, 2, KDEV, NEV), F32),
            pltpu.VMEM((SPIN, NSPACE, 2, KDEV, NEV), F32),
            pltpu.VMEM((SPIN, 2, NSPACE * KDEV, NEV), BF16),
            pltpu.VMEM((SPIN, 2, NSPACE * KDEV, NEV), BF16),
            pltpu.VMEM((2, BLOCK, BLOCK), F32),
            dma((NC,)),
            dma((2,)),
            dma((NMOM,)),
            dma((NMOM,)),
            dma((NMOM,)),
            dma((NMOM,)),
            dma((NMOM,)),
            dma((NMOM,)),
            dma((2,)),
            dma((2,)),
            dma((1,)),
            dma((1,)),
            dma((1,)),
            dma((1,)),
            dma((1,)),
            dma((2, NZ // 2, 2)),
            dma((1,)),
            dma((2, NZ // 2)),
            dma((1,)),
            dma((NZ,)),
            dma((1,)),
            dma((1,)),
            dma((1,)),
            dma((1,)),
            dma((3,)),
            dma((2,)),
        ],
        compiler_params=pltpu.CompilerParams(
            collective_id=0, has_side_effects=True, vmem_limit_bytes=48 * 2**20
        ),
    )(*(pltpu.with_memory_space_constraint(v, pltpu.HBM) for v in (momenta, graph_blocks.T, eig, perambulator)))
    norm = 1.0 / math.sqrt(NC * sites * NSPACE * 2 * NY)

    def finish(el_ref, own_ref, other_ref, el_out, sum_out, el_buf, own_buf, other_buf, sems):
        pairs = ((own_ref, own_buf), (other_ref, other_buf), (el_ref, el_buf))
        copies = [pltpu.make_async_copy(a, b, sems.at[k]) for k, (a, b) in enumerate(pairs)]
        for copy in copies:
            copy.start()
        copies[0].wait()
        copies[1].wait()
        own_buf[...] += other_buf[...]
        sum_copy = pltpu.make_async_copy(own_buf, sum_out, sems.at[3])
        sum_copy.start()
        copies[2].wait()
        el_buf[...] *= norm
        el_copy = pltpu.make_async_copy(el_buf, el_out, sems.at[4])
        el_copy.start()
        sum_copy.wait()
        el_copy.wait()

    anywhere = pl.BlockSpec(memory_space=pl.ANY)
    hbm = pl.BlockSpec(memory_space=pltpu.HBM)
    el, out = pl.pallas_call(
        finish,
        out_shape=(jax.ShapeDtypeStruct(el.shape, F32), jax.ShapeDtypeStruct(own.shape, F32)),
        in_specs=[anywhere] * 3,
        out_specs=(hbm, hbm),
        scratch_shapes=[
            pltpu.VMEM(el.shape, F32),
            pltpu.VMEM(own.shape, F32),
            pltpu.VMEM(own.shape, F32),
            dma((5,)),
        ],
        compiler_params=pltpu.CompilerParams(vmem_limit_bytes=8 * 2**20),
    )(el, own, other)
    return el.transpose(0, 1, 3, 2), out[None]


def solution(mesh):
    return jax.shard_map(
        per_device,
        mesh=mesh,
        in_specs=(P(None, None, None, ("space", "tile")), P(None, "space", None), P(), P()),
        out_specs=(P(None, None, "tile", "space"), P(("space", "tile"), None, None, None)),
        check_vma=False,
    )
```
